32 devices in a mesh: box: 8 (over z, x), dir: 4 (over y, core).
Axes of the slice: x: 2, y: 2, z: 4, core: 2. Of those that a mesh axis runs over, the one named last changes fastest.
Arguments:
- leaf_patterns: float32 [16, 16, 2, 64, 128], P('box', 'dir'), may hold values from -6 to 6
- occupancy: int32 [16], P('box'), may hold values from 0 to 16
- pair_lists: int32 [4, 1, 4], replicated, may hold values from 0 to 2, as said below
Outputs:
- translated: float32 [8, 1, 16, 2, 128, 512], P('box', None, None, None, 'dir')
The draws below stay inside these ranges and needn't reach their ends.
Inputs may be any that keep to these rules, and one draw needn't show every extreme that they name: `pair_lists`: each box's list names 4 source boxes, repeats allowed: positions 0 to 0 are the boxes of the pair before its own, 1 to 1 its own pair, the rest the pair after; never the box itself and never a pair outside 0 .. 3.
All inputs are finite; a program needn't handle non-finite values.
Results may differ from the reference program's by a relative error of at most 0.0003.
Values sent between devices are 32-bit elements; how exact they have to be, the bound alone decides.
A program may use at most 64 MiB of HBM per device.

```python
import jax
import jax.numpy as jnp
from jax import lax

LT = 64
LP = 128
RHS = 16
K = 4
LTR = 16
SLOTS = 1
N_LEAF = 16
PAIRS = 4
N_BOX = 8


def draw_leaf_patterns(key, part):
    noise_key, level_key = jax.random.split(key, 2)
    parity = (1 - 2 * (jnp.arange(LP, dtype=jnp.int32) % 2)).astype(jnp.float32)
    noise_part = 0.8 * jnp.clip(jax.random.normal(noise_key, (N_LEAF, RHS, 2, LT, LP), jnp.float32), -4.0, 4.0)
    level_part = jax.random.normal(level_key, (N_LEAF, RHS, 2, LT, 1), jnp.float32)
    return jnp.clip(noise_part + level_part * parity, -6.0, 6.0).astype(jnp.float32)


def draw_pair_lists(key, part):
    pair_numbers = jnp.arange(PAIRS, dtype=jnp.int32)[:, None, None]
    slot_numbers = jnp.arange(SLOTS, dtype=jnp.int32)[None, :, None]
    lowest = jnp.where(pair_numbers > 0, 0, SLOTS)
    highest_end = jnp.where(pair_numbers < PAIRS - 1, 3 * SLOTS, 2 * SLOTS)
    spread = highest_end - lowest - 1
    random_bits = jax.random.randint(key, (PAIRS, SLOTS, K), 0, 1 << 20, dtype=jnp.int32)
    chosen = lowest + random_bits % spread
    chosen = jnp.where(chosen >= SLOTS + slot_numbers, chosen + 1, chosen)
    chosen = chosen.at[1, 0, 0].set(3 * SLOTS - 1)
    chosen = chosen.at[1, 0, 1].set(0)
    return chosen.astype(jnp.int32)


def plant(drawn, key, smallest, high):
    longest = drawn.shape.index(max(drawn.shape))
    spots = []
    for shift in (0, 1):
        where = [jax.random.randint(jax.random.fold_in(key, axis), (), 0, length) for axis, length in enumerate(drawn.shape)]
        where[longest] = (where[longest] + shift) % drawn.shape[longest]
        spots.append(tuple(where))
    return drawn.at[spots[0]].set(smallest).at[spots[1]].set(high)


def setup_inputs(seed: int = 0) -> dict:
    key_list = jax.random.split(jax.random.key(seed), 4)
    return {
        "leaf_patterns": draw_leaf_patterns(jax.random.fold_in(key_list[3], 71), 0),
        "occupancy": plant(jax.random.randint(key_list[1], (N_LEAF,), 0, 17), jax.random.fold_in(key_list[1], 1), 0, 16).astype(jnp.int32),
        "pair_lists": draw_pair_lists(jax.random.fold_in(key_list[3], 71), 0),
    }


full_count = 16.0
phase_first = 16.0
phase_second = 64.0
translate_wave = 20.0
highest = lax.Precision.HIGHEST

def interp_table(points, offset):
    mode_count = points // 2
    orders = jnp.arange(mode_count + 1, dtype=jnp.float32)
    weights = jnp.where((orders == 0) | (orders == mode_count), 1.0, 2.0) / points
    source = (jnp.arange(points, dtype=jnp.float32) + offset) / points
    target = (jnp.arange(2 * points, dtype=jnp.float32) + offset) / (2 * points)
    source_angle = 2.0 * jnp.pi * source[:, None] * orders[None, :]
    target_angle = 2.0 * jnp.pi * target[:, None] * orders[None, :]
    return jnp.dot(jnp.cos(target_angle) * weights, jnp.cos(source_angle).T, precision=highest) + jnp.dot(jnp.sin(target_angle) * weights, jnp.sin(source_angle).T, precision=highest)

def directions(row_numbers, rows_total, columns):
    theta_rows = (jnp.pi * (row_numbers.astype(jnp.float32) + 0.5) / rows_total)[:, None]
    azimuth = 2.0 * jnp.pi / columns * jnp.arange(columns, dtype=jnp.float32)[None, :]
    sine_theta = jnp.sin(theta_rows)
    return (sine_theta * jnp.cos(azimuth), sine_theta * jnp.sin(azimuth), jnp.cos(theta_rows) * jnp.ones_like(azimuth))

def interpolate(pattern, row_table, column_table):
    rows_done = jnp.einsum('it,...tp->...ip', row_table, pattern, precision=highest)
    return jnp.einsum('...ip,qp->...iq', rows_done, column_table, precision=highest)

def apply_phase(pattern, angles):
    real_part = pattern[..., 0, :, :]
    imag_part = pattern[..., 1, :, :]
    cosine = jnp.cos(angles)
    sine_value = jnp.sin(angles)
    return jnp.stack([real_part * cosine - imag_part * sine_value, real_part * sine_value + imag_part * cosine], axis=-3)

def contribute(child_pattern, child_sign, row_start, row_count, row_table, column_table, wave_scale, component):
    rows_used = lax.dynamic_slice_in_dim(row_table, row_start, row_count, 0)
    row_numbers = row_start + jnp.arange(row_count, dtype=jnp.int32)
    along_x, along_y, along_z = directions(row_numbers, row_table.shape[0], column_table.shape[0])
    picked_axis = along_x if component == 0 else along_y
    angles = picked_axis * (wave_scale * child_sign)
    return apply_phase(interpolate(child_pattern, rows_used, column_table), angles)

def box_center(numbers):
    return jnp.stack([numbers % 4, numbers // 4 % 4, numbers // 16], axis=-1).astype(jnp.float32)

def translation_table(offsets, along_x, along_y, along_z):
    distance = jnp.sqrt(lax.optimization_barrier(jnp.sum(offsets * offsets, axis=1)))
    unit_vector = offsets / distance[:, None]
    cosine = unit_vector[:, 0, None, None] * along_x[None] + unit_vector[:, 1, None, None] * along_y[None] + unit_vector[:, 2, None, None] * along_z[None]
    argument = (translate_wave * distance)[:, None, None]
    sine_arg = jnp.sin(argument)
    cosine_arg = jnp.cos(argument)
    squared = argument * argument
    hankel_now = (sine_arg / argument, -cosine_arg / argument)
    hankel_next = ((sine_arg - argument * cosine_arg) / squared, -(argument * sine_arg + cosine_arg) / squared)
    legendre_now = jnp.ones_like(cosine)
    legendre_next = cosine
    summed_real = jnp.zeros_like(cosine)
    summed_imag = jnp.zeros_like(cosine)
    for degree in range(LTR + 1):
        weight_now = (2.0 * degree + 1.0) * legendre_now
        real_now, imag_now = hankel_now
        if degree % 4 == 0:
            turned = (real_now, imag_now)
        elif degree % 4 == 1:
            turned = (-imag_now, real_now)
        elif degree % 4 == 2:
            turned = (-real_now, -imag_now)
        else:
            turned = (imag_now, -real_now)
        summed_real = summed_real + weight_now * turned[0]
        summed_imag = summed_imag + weight_now * turned[1]
        factor = (2.0 * degree + 3.0) / argument
        hankel_now, hankel_next = (hankel_next, (factor * hankel_next[0] - hankel_now[0], factor * hankel_next[1] - hankel_now[1]))
        legendre_now, legendre_next = (legendre_next, ((2.0 * degree + 3.0) * cosine * legendre_next - (degree + 1.0) * legendre_now) / (degree + 2.0))
    return jnp.stack([summed_real, summed_imag], axis=1) / offsets.shape[0]

def complex_sum(operator_table, picked):
    table_real = operator_table[:, 0][:, None]
    table_imag = operator_table[:, 1][:, None]
    source_real = picked[:, :, 0]
    source_imag = picked[:, :, 1]
    return jnp.stack([lax.optimization_barrier(jnp.sum(table_real * source_real - table_imag * source_imag, axis=0)), lax.optimization_barrier(jnp.sum(table_real * source_imag + table_imag * source_real, axis=0))], axis=1)

def reference(leaf_patterns, occupancy, pair_lists):
    weighted = leaf_patterns * (occupancy.astype(jnp.float32) / full_count)[:, None, None, None, None]
    first_rows = interp_table(LT, 0.5)
    first_columns = interp_table(LP, 0.0)
    second_rows = interp_table(2 * LT, 0.5)
    second_columns = interp_table(2 * LP, 0.0)

    def merge_first(number):
        pair_leaves = lax.dynamic_slice_in_dim(weighted, 2 * number, 2, 0)
        summed = contribute(pair_leaves[0], -1.0, 0, 2 * LT, first_rows, first_columns, phase_first, 0)
        return summed + contribute(pair_leaves[1], 1.0, 0, 2 * LT, first_rows, first_columns, phase_first, 0)
    first_level = lax.map(merge_first, jnp.arange(N_LEAF // 2, dtype=jnp.int32))

    def merge_second(number):
        pair_id = number // SLOTS
        slot_id = number % SLOTS
        lower_child = lax.dynamic_index_in_dim(first_level, 2 * pair_id * SLOTS + slot_id, 0, keepdims=False)
        upper_child = lax.dynamic_index_in_dim(first_level, (2 * pair_id + 1) * SLOTS + slot_id, 0, keepdims=False)
        summed = contribute(lower_child, -1.0, 0, 4 * LT, second_rows, second_columns, phase_second, 1)
        return summed + contribute(upper_child, 1.0, 0, 4 * LT, second_rows, second_columns, phase_second, 1)
    second_level = lax.map(merge_second, jnp.arange(PAIRS * SLOTS, dtype=jnp.int32))
    along_x, along_y, along_z = directions(jnp.arange(4 * LT, dtype=jnp.int32), 4 * LT, 4 * LP)

    def translate(number):
        pair_id = number // SLOTS
        slot_id = number % SLOTS
        chosen = pair_lists[pair_id, slot_id]
        source_ids = pair_id * SLOTS - SLOTS + chosen
        offsets = box_center(number)[None, :] - box_center(source_ids)
        operator_table = translation_table(offsets, along_x, along_y, along_z)
        picked = jnp.take(second_level, source_ids, axis=0)
        return complex_sum(operator_table, picked)
    incoming = lax.map(translate, jnp.arange(PAIRS * SLOTS, dtype=jnp.int32))
    shaped = incoming.reshape(PAIRS, SLOTS, RHS, 2, 2, 2 * LT, 4 * LP).transpose(0, 4, 1, 2, 3, 5, 6)
    return shaped.reshape(N_BOX, SLOTS, RHS, 2, 2 * LT, 4 * LP)
```

```python
import functools

import jax
import jax.numpy as jnp
import numpy as np
from jax import lax
from jax.experimental import pallas as pl
from jax.experimental.pallas import tpu as pltpu
from jax.sharding import PartitionSpec as P

MESH = pl.DeviceIdType.MESH
LTR = 16
full_count = 16.0
phase_first = 16.0
phase_second = 64.0
translate_wave = 20.0


def interp_table(points, offset):
    orders = np.arange(points // 2 + 1, dtype=np.float64)
    weights = np.where((orders == 0) | (orders == points // 2), 1.0, 2.0) / points
    source = (np.arange(points) + offset) / points
    target = (np.arange(2 * points) + offset) / (2 * points)
    angle = 2.0 * np.pi * (target[:, None, None] - source[None, :, None]) * orders
    return (np.cos(angle) * weights).sum(-1)


def halves(table):
    high = np.asarray(table, np.float32).astype(jnp.bfloat16)
    low = (np.asarray(table, np.float64) - high.astype(np.float64)).astype(jnp.bfloat16)
    return high, low


def sines(rows, columns):
    theta = np.pi * (np.arange(rows) + 0.5) / rows
    phi = 2.0 * np.pi * np.arange(columns) / columns
    return np.sin(theta), np.cos(theta), np.cos(phi), np.sin(phi)


def center(g):
    return np.array([g % 4, g // 4 % 4, g // 16], np.float64)


def series_table(pairs):
    table = np.zeros((pairs, 2 * (3 + 2 * (LTR + 1))), np.float64)
    width = 3 + 2 * (LTR + 1)
    for g in range(pairs):
        for side, s in enumerate((g - 1, g + 1)):
            if not 0 <= s < pairs:
                continue
            r = center(g) - center(s)
            distance = np.sqrt((r * r).sum())
            x = translate_wave * distance
            now = (np.sin(x) - 1j * np.cos(x)) / x
            nxt = ((np.sin(x) - x * np.cos(x)) - 1j * (x * np.sin(x) + np.cos(x))) / x**2
            table[g, side * width : side * width + 3] = r / distance
            for degree in range(LTR + 1):
                value = (1j**degree) * (2 * degree + 1) * now
                table[g, side * width + 3 + 2 * degree] = value.real
                table[g, side * width + 4 + 2 * degree] = value.imag
                now, nxt = nxt, (2 * degree + 3) / x * nxt - now
    return table.astype(np.float32)


def split(value):
    high = value.astype(jnp.bfloat16)
    low = (value - high.astype(jnp.float32)).astype(jnp.bfloat16)
    return high, low


def dot(a, b):
    return jnp.dot(a, b, preferred_element_type=jnp.float32)


def kernel(
    sizes,
    leaf_in, occ_in, lists_in, series_in, c1_in, r1_in, r2_in, c2_in, ph1_in, ph2_in,
    polar_in, azim_in, turn_in,
    out,
    leaf, occ, lists, series, c1, r1, r2, c2, ph1, ph2, polar, azim, turn,
    mine, gath, taken, lhs2, even, ready, oper,
    loads, xs, xr, ls, lr, ys, ds, dr,
):
    n_box, n_dir, count, lt, lp, slab, crossed = sizes
    plain = count - 2 * crossed
    half_n = n_dir // 2
    rows = 2 * lt
    box = lax.axis_index("box")
    me = lax.axis_index("dir")
    x = box % 2
    pair = box // 2
    dh = me // half_n
    dl = me % half_n
    has_lower = pair > 0
    has_upper = pair < n_box // 2 - 1
    partner = box + 1 - 2 * x
    across = (me + half_n) % n_dir

    barrier = pltpu.get_barrier_semaphore()
    for o in range(1, n_dir):
        pl.semaphore_signal(
            barrier, inc=1, device_id=(box, (me + o) % n_dir), device_id_type=MESH
        )
    if crossed:
        for k in range(half_n):
            pl.semaphore_signal(
                barrier, inc=1, device_id=(partner, dh * half_n + k), device_id_type=MESH
            )
    else:
        pl.semaphore_signal(barrier, inc=1, device_id=(partner, me), device_id_type=MESH)
    for present, by in ((has_lower, -2), (has_upper, 2)):
        @pl.when(present)
        def _():
            pl.semaphore_signal(barrier, inc=1, device_id=(box + by, me), device_id_type=MESH)

    start_own = pl.multiple_of(x * rows, rows)
    pairs_in = [
        (leaf_in, leaf), (occ_in, occ), (turn_in, turn), (lists_in, lists), (series_in, series),
        (polar_in, polar), (azim_in, azim), (c1_in, c1), (r1_in, r1),
        (ph1_in, ph1), (c2_in, c2), (ph2_in, ph2),
        (r2_in.at[pl.ds(start_own, rows)], r2.at[0]),
    ]
    if crossed:
        for k in range(2):
            start = pl.multiple_of(k * rows + dh * lt, lt)
            pairs_in.append((r2_in.at[pl.ds(start, lt)], r2.at[1, pl.ds(k * lt, lt)]))
    copies = [
        pltpu.make_async_copy(source, target, loads.at[i])
        for i, (source, target) in enumerate(pairs_in)
    ]
    for copy in copies:
        copy.start()
    for copy in copies[:3]:
        copy.wait()

    w0 = occ[0].astype(jnp.float32) / full_count
    w1 = occ[1].astype(jnp.float32) / full_count
    turned = jnp.broadcast_to(turn[...], (lt, lp))
    for r in range(count):
        for c in range(2):
            a = jnp.take_along_axis(leaf[0, r, c], turned, axis=1) * w0
            b = jnp.take_along_axis(leaf[1, r, c], turned, axis=1) * w1
            mine[r, c] = a + b
            mine[r, 2 + c] = b - a

    pl.semaphore_wait(
        barrier,
        n_dir - 1 + (half_n if crossed else 1)
        + has_lower.astype(jnp.int32) + has_upper.astype(jnp.int32),
    )

    def x_copy(i):
        source = mine.at[i] if i < plain else mine.at[plain + 1 - x]
        return pltpu.make_async_remote_copy(
            source, gath.at[i], xs.at[i], xr.at[i], (partner, me), device_id_type=MESH
        )

    def z_copy(i, passed, side):
        if passed:
            source = gath.at[i]
            place = 1 - x
        else:
            source = mine.at[i] if i < plain else mine.at[plain + x]
            place = x
        unit = i if i < plain else plain + dh
        return pltpu.make_async_remote_copy(
            source, taken.at[side, unit, place], ls.at[side, i, passed],
            lr.at[side, unit, place], (box + 2 - 4 * side, me), device_id_type=MESH,
        )

    def z_start(i, passed):
        @pl.when(has_upper)
        def _():
            z_copy(i, passed, 0).start()

        @pl.when(has_lower)
        def _():
            z_copy(i, passed, 1).start()

    def arrived(side, unit, place):
        pltpu.make_async_remote_copy(
            mine.at[0], taken.at[side, unit, place], ls.at[side, 0, 0],
            lr.at[side, unit, place], (partner, me), device_id_type=MESH,
        ).wait_recv()

    def y_copy(side, passed):
        place = 1 - x if passed else x
        block = taken.at[side, plain + dh, place]
        return pltpu.make_async_remote_copy(
            block, block, ys.at[side, passed], lr.at[side, plain + dh, place],
            (box, across), device_id_type=MESH,
        )

    def y_start(passed):
        for side, present in ((0, has_lower), (1, has_upper)):
            @pl.when(present)
            def _():
                arrived(side, plain + dh, 1 - x if passed else x)
                y_copy(side, passed).start()

    if crossed:
        x_copy(plain).start()
        z_start(plain, 0)
    for i in range(plain):
        x_copy(i).start()
    if not crossed:
        z_start(0, 0)

    for side, present in ((0, has_lower), (1, has_upper)):
        @pl.when(jnp.logical_not(present))
        def _():
            taken[side] = jnp.zeros(taken.shape[1:], jnp.float32)

    for copy in copies[3:7]:
        copy.wait()

    slots = lists.shape[1]
    entries = lists.shape[2]
    width = 3 + 2 * (LTR + 1)
    blocks = rows // 8
    for side, present in ((0, has_lower), (1, has_upper)):
        named = jnp.float32(0.0)
        for k in range(entries):
            chosen = lists[pair, 0, k]
            hit = chosen < slots if side == 0 else chosen >= 2 * slots
            named = named + jnp.where(hit, 1.0, 0.0)
        scale = named / entries
        base = side * width

        def oper_step(i, carry):
            other = i // blocks
            start = (x + other) % 2 * rows + other * dh * lt + i % blocks * 8
            at = pl.ds(pl.multiple_of(start, 8), 8)
            along_x = polar[0, at] * azim[0:1]
            along_y = polar[0, at] * azim[1:2]
            along_z = polar[1, at] * jnp.ones_like(along_x)
            u = (
                series[pair, base] * along_x
                + series[pair, base + 1] * along_y
                + series[pair, base + 2] * along_z
            )
            now, nxt = jnp.ones_like(u), u
            real, imag = jnp.zeros_like(u), jnp.zeros_like(u)
            for degree in range(LTR + 1):
                real = real + series[pair, base + 3 + 2 * degree] * now
                imag = imag + series[pair, base + 4 + 2 * degree] * now
                now, nxt = nxt, (
                    ((2.0 * degree + 3.0) / (degree + 2.0)) * (u * nxt)
                    - ((degree + 1.0) / (degree + 2.0)) * now
                )
            oper[side, 0, at] = real * scale
            oper[side, 1, at] = imag * scale
            return carry

        lax.fori_loop(0, blocks + (lt // 8 if crossed else 0), oper_step, 0)

    for copy in copies[7:]:
        copy.wait()

    if crossed:
        x_copy(plain).wait_recv()
        z_start(plain, 1)
        z_start(0, 0)
        y_start(0)
        x_copy(0).wait_recv()
        z_start(0, 1)
        if plain > 1:
            z_start(1, 0)
        y_start(1)

    lanes = lax.broadcasted_iota(jnp.int32, (slab, lp), 1)
    odd_lane = lanes % 2 == 1
    late_lane = lanes % 4 >= 2

    def woven(planes):
        pairs = [jnp.where(odd_lane, planes[(k + 1) % 4], planes[k]) for k in range(4)]
        mixed = [jnp.where(late_lane, pairs[(2 - h) % 4], pairs[-h % 4]) for h in range(4)]
        return [mixed[h] if h == 0 else pltpu.roll(mixed[h], lp - h, 1) for h in range(4)]

    def first_level(unit, side):
        source = jnp.concatenate(
            [taken[side, unit, place].reshape(4 * lt, lp) for place in range(2)], axis=0
        )
        high, low = split(source)
        both = dot(jnp.concatenate([high, low], axis=1), c1[...])
        odd_high, odd_low = split(both[:, :lp] + both[:, lp:])
        high = jnp.concatenate([high, odd_high], axis=1)
        low = jnp.concatenate([low, odd_low], axis=1)
        done = []
        cosine, sine = ph1[0], ph1[1]
        for place in range(2):
            parts = []
            for k in range(4):
                at = slice((4 * place + k) * lt, (4 * place + k + 1) * lt)
                parts.append(
                    dot(r1[...], jnp.concatenate([high[at], low[at], high[at]], axis=0))
                )
            sr, si, dre, dim = parts
            done.append((cosine * sr - sine * dim, cosine * si + sine * dre))
        return done

    def unit_at(step):
        if not crossed:
            return 0, step
        kind = 1 - step % 2
        return kind, kind * (plain + (dh + step // 2) % 2) + (1 - kind) * (step // 2)

    def slab_at(kind, s):
        if not crossed:
            return box, s, x * rows + s * slab
        top = s // half_n
        low = s % half_n
        to_box = kind * (pair * 2 + top) + (1 - kind) * box
        to_dir = kind * (dh * half_n + low) + (1 - kind) * s
        row = kind * (top * rows + dh * lt + low * slab) + (1 - kind) * (x * rows + s * slab)
        return to_box, to_dir, row

    def own_slab(kind):
        return kind * (x * half_n + dl) + (1 - kind) * me

    def whose(kind, unit):
        if not crossed:
            return me * count + unit
        source = (unit - plain) * half_n + dl
        return kind * (source * count + plain + x) + (1 - kind) * (me * count + unit)

    def d_copy(kind, unit, o):
        s = (own_slab(kind) + o) % n_dir
        to_box, to_dir, _ = slab_at(kind, s)
        rhs = whose(kind, unit)
        return pltpu.make_async_remote_copy(
            ready.at[unit, s], out.at[rhs], ds.at[unit, o], dr.at[rhs],
            (to_box, to_dir), device_id_type=MESH,
        )

    def do_unit(kind, unit):
        for side in range(2):
            (ar, ai), (br, bi) = first_level(unit, side)
            for k, value in enumerate((ar + br, ai + bi, br - ar, bi - ai)):
                high, low = split(value)
                wide = dot(r2[kind], jnp.concatenate([high, low, high], axis=0))
                even[side, k] = wide
                high, low = split(wide)
                lhs2[side, k, :, : 2 * lp] = high
                lhs2[side, k, :, 2 * lp :] = low
        for o in range(1, n_dir + 1):
            s = (own_slab(kind) + o) % n_dir
            at = pl.ds(pl.multiple_of(s * slab, slab), slab)
            both = jnp.concatenate(
                [lhs2[side, k, at, :] for side in range(2) for k in range(4)], axis=0
            )
            odd = dot(jnp.concatenate([both, both[:, : 2 * lp]], axis=1), c2[...])
            row = pl.ds(pl.multiple_of(slab_at(kind, s)[2], slab), slab)
            planes = []
            for v in range(4):
                cut = slice(v * lp, (v + 1) * lp)
                cosine, sine = ph2[0, row, cut], ph2[1, row, cut]
                total = None
                for side in range(2):
                    if v < 2:
                        sr, si, dre, dim = [even[side, k, at, cut] for k in range(4)]
                    else:
                        sr, si, dre, dim = [
                            odd[(4 * side + k) * slab : (4 * side + k + 1) * slab,
                                (v - 2) * lp : (v - 1) * lp]
                            for k in range(4)
                        ]
                    gr = cosine * sr - sine * dim
                    gi = cosine * si + sine * dre
                    pr, pi = oper[side, 0, row, cut], oper[side, 1, row, cut]
                    real, imag = pr * gr - pi * gi, pr * gi + pi * gr
                    total = (real, imag) if total is None else (total[0] + real, total[1] + imag)
                planes.append(total)
            for c in range(2):
                parts = woven([planes[v][c] for v in (0, 2, 1, 3)])
                for h in range(4):
                    ready[unit, s, c, :, h * lp : (h + 1) * lp] = parts[h]
            if o < n_dir:
                d_copy(kind, unit, o).start()
            else:
                out[whose(kind, unit)] = ready[unit, s]

    def level_step(step, carry):
        kind, unit = unit_at(step)
        if crossed:
            if plain > 1:
                @pl.when(step == 1)
                def _():
                    x_copy(1).wait_recv()
                    z_start(1, 1)
        else:
            for i in range(plain):
                @pl.when(step == i)
                def _():
                    if i > 0:
                        z_start(i, 0)
                    x_copy(i).wait_recv()
                    z_start(i, 1)

        for side, present in ((0, has_lower), (1, has_upper)):
            @pl.when(jnp.logical_and(present, step >= crossed))
            def _():
                for place in range(2):
                    arrived(side, unit, place)

        do_unit(kind, unit)
        return carry

    lax.fori_loop(0, count, level_step, 0)

    def out_arrived(rhs):
        pltpu.make_async_remote_copy(
            ready.at[0, 0], out.at[rhs], ds.at[0, 0], dr.at[rhs],
            (box, across), device_id_type=MESH,
        ).wait_recv()

    for step in range(count):
        kind, unit = unit_at(step)
        for o in range(1, n_dir):
            d_copy(kind, unit, o).wait_send()
    for o in range(1, n_dir):
        for r in range(plain):
            out_arrived((me + o) % n_dir * count + r)
        if crossed:
            s = (x * half_n + dl + o) % n_dir
            for k in range(2):
                out_arrived((k * half_n + s % half_n) * count + plain + s // half_n)
    for i in range(plain + crossed):
        x_copy(i).wait_send()
    for side, sends, gets in ((0, has_upper, has_lower), (1, has_lower, has_upper)):
        @pl.when(sends)
        def _():
            for i in range(plain + crossed):
                for passed in range(2):
                    z_copy(i, passed, side).wait_send()

        if crossed:
            @pl.when(gets)
            def _():
                for passed in range(2):
                    y_copy(side, passed).wait_send()


def per_device(n_box, n_dir, leaf_patterns, occupancy, pair_lists):
    _, count, _, lt, lp = leaf_patterns.shape
    assert leaf_patterns.shape[0] == 2
    slab = 2 * lt // n_dir
    crossed = int(count >= 4 and n_dir % 2 == 0)
    steps = count - crossed
    bf16 = jnp.bfloat16
    lane = np.arange(lp)
    order = []
    for s in range(4):
        h = (lane % 4 - s) % 4
        order.append(lp * h + (lane - h) % lp)
    turn = (order[0] // 4).astype(np.int32)[None]
    first_order = np.concatenate([order[0], order[2]]) // 2
    second_odd = np.concatenate([order[1], order[3]])
    second_order = np.concatenate([order[0], order[2], second_odd])
    high, low = halves(interp_table(lp, 0.0)[first_order[lp:]][:, turn[0]].T)
    c1 = np.concatenate([np.concatenate([high, low], axis=1)] * 2, axis=0)
    row_high, row_low = halves(interp_table(lt, 0.5))
    r1 = np.concatenate([row_high, row_high, row_low], axis=1)
    row_high, row_low = halves(interp_table(2 * lt, 0.5))
    r2 = np.concatenate([row_high, row_high, row_low], axis=1)
    high, low = halves(interp_table(2 * lp, 0.0)[second_odd][:, first_order].T)
    c2 = np.concatenate([high, high, low], axis=0)
    st, _, cp, _ = sines(2 * lt, 2 * lp)
    angle = phase_first * st[:, None] * cp[first_order][None]
    ph1 = np.stack([np.cos(angle), np.sin(angle)]).astype(np.float32)
    st, ct, cp, sp = sines(4 * lt, 4 * lp)
    cp, sp = cp[second_order], sp[second_order]
    angle = phase_second * st[:, None] * sp[None]
    ph2 = np.stack([np.cos(angle), np.sin(angle)]).astype(np.float32)
    polar = np.stack([st, ct])[:, :, None].astype(np.float32)
    azim = np.stack([cp, sp]).astype(np.float32)
    series = series_table(n_box // 2)
    operands = (
        leaf_patterns, occupancy, pair_lists, series, c1, r1, r2, c2, ph1, ph2, polar, azim,
        turn,
    )
    chunk = (2, slab, 4 * lp)
    f32 = jnp.float32
    rows = 2 * lt
    result = pl.pallas_call(
        functools.partial(kernel, (n_box, n_dir, count, lt, lp, slab, crossed)),
        out_shape=jax.ShapeDtypeStruct((n_dir * count,) + chunk, f32),
        in_specs=[pl.BlockSpec(memory_space=pltpu.HBM)] * len(operands),
        out_specs=pl.BlockSpec(memory_space=pltpu.VMEM),
        scratch_shapes=[
            pltpu.VMEM(leaf_patterns.shape, f32),
            pltpu.SMEM(occupancy.shape, jnp.int32),
            pltpu.SMEM(pair_lists.shape, jnp.int32),
            pltpu.SMEM(series.shape, f32),
            pltpu.VMEM(c1.shape, bf16),
            pltpu.VMEM(r1.shape, bf16),
            pltpu.VMEM((1 + crossed, rows) + r2.shape[1:], bf16),
            pltpu.VMEM(c2.shape, bf16),
            pltpu.VMEM(ph1.shape, f32),
            pltpu.VMEM(ph2.shape, f32),
            pltpu.VMEM(polar.shape, f32),
            pltpu.VMEM(azim.shape, f32),
            pltpu.VMEM(turn.shape, jnp.int32),
            pltpu.VMEM((count, 4, lt, lp), f32),
            pltpu.VMEM((steps, 4, lt, lp), f32),
            pltpu.VMEM((2, count, 2, 4, lt, lp), f32),
            pltpu.VMEM((2, 4, rows, 4 * lp), bf16),
            pltpu.VMEM((2, 4, rows, 2 * lp), f32),
            pltpu.VMEM((count, n_dir) + chunk, f32),
            pltpu.VMEM((2, 2, 2 * rows, 4 * lp), f32),
            pltpu.SemaphoreType.DMA((len(operands) + 2 * crossed,)),
            pltpu.SemaphoreType.DMA((steps,)),
            pltpu.SemaphoreType.DMA((steps,)),
            pltpu.SemaphoreType.DMA((2, steps, 2)),
            pltpu.SemaphoreType.DMA((2, count, 2)),
            pltpu.SemaphoreType.DMA((2, 2)),
            pltpu.SemaphoreType.DMA((count, n_dir)),
            pltpu.SemaphoreType.DMA((n_dir * count,)),
        ],
        compiler_params=pltpu.CompilerParams(
            collective_id=0, has_side_effects=True, vmem_limit_bytes=48 << 20
        ),
    )(*[pltpu.with_memory_space_constraint(jnp.asarray(operand), pltpu.HBM) for operand in operands])
    return result.reshape(1, 1, n_dir * count, *chunk)


def solution(mesh):
    placed = (P("box", "dir", None, None, None), P("box"), P())
    return jax.shard_map(
        functools.partial(per_device, mesh.shape["box"], mesh.shape["dir"]),
        mesh=mesh,
        in_specs=placed,
        out_specs=P("box", None, None, None, "dir", None),
        check_vma=False,
    )
```

```python
import functools

import jax
import jax.numpy as jnp
import numpy as np
from jax import lax
from jax.experimental import pallas as pl
from jax.experimental.pallas import tpu as pltpu
from jax.sharding import PartitionSpec as P

MESH = pl.DeviceIdType.MESH
LTR = 16
full_count = 16.0
phase_first = 16.0
phase_second = 64.0
translate_wave = 20.0


def interp_table(points, offset):
    orders = np.arange(points // 2 + 1, dtype=np.float64)
    weights = np.where((orders == 0) | (orders == points // 2), 1.0, 2.0) / points
    source = (np.arange(points) + offset) / points
    target = (np.arange(2 * points) + offset) / (2 * points)
    angle = 2.0 * np.pi * (target[:, None, None] - source[None, :, None]) * orders
    return (np.cos(angle) * weights).sum(-1)


def halves(table):
    high = np.asarray(table, np.float32).astype(jnp.bfloat16)
    low = (np.asarray(table, np.float64) - high.astype(np.float64)).astype(jnp.bfloat16)
    return high, low


def sines(rows, columns):
    theta = np.pi * (np.arange(rows) + 0.5) / rows
    phi = 2.0 * np.pi * np.arange(columns) / columns
    return np.sin(theta), np.cos(theta), np.cos(phi), np.sin(phi)


def center(g):
    return np.array([g % 4, g // 4 % 4, g // 16], np.float64)


def series_table(pairs):
    table = np.zeros((pairs, 2 * (3 + 2 * (LTR + 1))), np.float64)
    width = 3 + 2 * (LTR + 1)
    for g in range(pairs):
        for side, s in enumerate((g - 1, g + 1)):
            if not 0 <= s < pairs:
                continue
            r = center(g) - center(s)
            distance = np.sqrt((r * r).sum())
            x = translate_wave * distance
            now = (np.sin(x) - 1j * np.cos(x)) / x
            nxt = ((np.sin(x) - x * np.cos(x)) - 1j * (x * np.sin(x) + np.cos(x))) / x**2
            table[g, side * width : side * width + 3] = r / distance
            for degree in range(LTR + 1):
                value = (1j**degree) * (2 * degree + 1) * now
                table[g, side * width + 3 + 2 * degree] = value.real
                table[g, side * width + 4 + 2 * degree] = value.imag
                now, nxt = nxt, (2 * degree + 3) / x * nxt - now
    return table.astype(np.float32)


def split(value):
    high = value.astype(jnp.bfloat16)
    low = (value - high.astype(jnp.float32)).astype(jnp.bfloat16)
    return high, low


def dot(a, b):
    return jnp.dot(a, b, preferred_element_type=jnp.float32)


def kernel(
    sizes,
    leaf_in, occ_in, lists_in, series_in, c1_in, r1_in, r2_in, c2_in, ph1_in, ph2_in,
    polar_in, azim_in, turn_in,
    out,
    leaf, occ, lists, series, c1, r1, r2, c2, ph1, ph2, polar, azim, turn,
    mine, gath, yours, taken, first, lhs2, even, ready, oper,
    loads, xs, xr, ls, lr, ys, ds, dr,
):
    n_box, n_dir, count, lt, lp, slab, crossed = sizes
    plain = count - 2 * crossed
    half_n = n_dir // 2
    rows = 2 * lt
    box = lax.axis_index("box")
    me = lax.axis_index("dir")
    x = box % 2
    pair = box // 2
    dh = me // half_n
    dl = me % half_n
    turned_order = 0 * dl
    has_lower = pair > 0
    has_upper = pair < n_box // 2 - 1
    partner = box + 1 - 2 * x
    across = (me + half_n) % n_dir

    barrier = pltpu.get_barrier_semaphore()
    for o in range(1, n_dir):
        pl.semaphore_signal(
            barrier, inc=1, device_id=(box, (me + o) % n_dir), device_id_type=MESH
        )
    if crossed:
        for k in range(half_n):
            pl.semaphore_signal(
                barrier, inc=1, device_id=(partner, dh * half_n + k), device_id_type=MESH
            )
        for present, by in ((has_lower, -2), (has_upper, 2)):
            @pl.when(present)
            def _():
                pl.semaphore_signal(
                    barrier, inc=1, device_id=(partner + by, me), device_id_type=MESH
                )
    else:
        pl.semaphore_signal(barrier, inc=1, device_id=(partner, me), device_id_type=MESH)
    for present, by in ((has_lower, -2), (has_upper, 2)):
        @pl.when(present)
        def _():
            pl.semaphore_signal(barrier, inc=1, device_id=(box + by, me), device_id_type=MESH)

    start_own = pl.multiple_of(x * rows, rows)
    pairs_in = [
        (leaf_in, leaf), (occ_in, occ), (turn_in, turn), (lists_in, lists), (series_in, series),
        (polar_in, polar), (azim_in, azim), (c1_in, c1), (r1_in, r1),
        (ph1_in, ph1), (c2_in, c2), (ph2_in, ph2),
        (r2_in.at[pl.ds(start_own, rows)], r2.at[0]),
    ]
    if crossed:
        for k in range(2):
            start = pl.multiple_of(k * rows + dh * lt, lt)
            pairs_in.append((r2_in.at[pl.ds(start, lt)], r2.at[1, pl.ds(k * lt, lt)]))
    copies = [
        pltpu.make_async_copy(source, target, loads.at[i])
        for i, (source, target) in enumerate(pairs_in)
    ]
    for copy in copies:
        copy.start()
    for copy in copies[:3]:
        copy.wait()

    w0 = occ[0].astype(jnp.float32) / full_count
    w1 = occ[1].astype(jnp.float32) / full_count
    turned = jnp.broadcast_to(turn[...], (lt, lp))
    for r in range(count):
        for c in range(2):
            a = jnp.take_along_axis(leaf[0, r, c], turned, axis=1) * w0
            b = jnp.take_along_axis(leaf[1, r, c], turned, axis=1) * w1
            mine[r, c] = a + b
            mine[r, 2 + c] = b - a

    pl.semaphore_wait(
        barrier,
        n_dir - 1 + (half_n if crossed else 1)
        + (1 + crossed) * (has_lower.astype(jnp.int32) + has_upper.astype(jnp.int32)),
    )

    def x_copy(i):
        return pltpu.make_async_remote_copy(
            mine.at[i], gath.at[i], xs.at[i], xr.at[i], (partner, me), device_id_type=MESH
        )

    def z_copy(i, passed, side):
        by = 2 - 4 * side
        target = box + by
        if i == plain:
            unit = plain + dh
            source, place = mine.at[plain + x], x
            if passed == 1:
                source, target = mine.at[plain + 1 - x], partner + by
            elif passed == 2:
                source, unit = yours, plain + 1 - dh
        else:
            unit = i
            source, place = (gath.at[i], 1 - x) if passed else (mine.at[i], x)
        return pltpu.make_async_remote_copy(
            source, taken.at[side, unit, place], ls.at[side, i, passed],
            lr.at[side, unit, place], (target, me), device_id_type=MESH,
        )

    def z_start(i, passed):
        @pl.when(has_upper)
        def _():
            z_copy(i, passed, 0).start()

        @pl.when(has_lower)
        def _():
            z_copy(i, passed, 1).start()

    def arrived(side, unit, place):
        pltpu.make_async_remote_copy(
            mine.at[0], taken.at[side, unit, place], ls.at[side, 0, 0],
            lr.at[side, unit, place], (partner, me), device_id_type=MESH,
        ).wait_recv()

    def y_first():
        return pltpu.make_async_remote_copy(
            mine.at[plain + x], yours, ys.at[2], ys.at[3], (box, across),
            device_id_type=MESH,
        )

    def y_copy(side):
        block = taken.at[side, plain + dh, 1 - x]
        return pltpu.make_async_remote_copy(
            block, block, ys.at[side], lr.at[side, plain + dh, 1 - x],
            (box, across), device_id_type=MESH,
        )

    def y_start():
        for side, present in ((0, has_lower), (1, has_upper)):
            @pl.when(present)
            def _():
                arrived(side, plain + dh, 1 - x)
                y_copy(side).start()

    if crossed:
        y_first().start()
        x_copy(0).start()
        z_start(plain, 0)
        z_start(plain, 1)
        z_start(0, 0)
        for i in range(1, plain):
            x_copy(i).start()
    else:
        for i in range(plain):
            x_copy(i).start()
            z_start(i, 0)

    for side, present in ((0, has_lower), (1, has_upper)):
        @pl.when(jnp.logical_not(present))
        def _():
            taken[side] = jnp.zeros(taken.shape[1:], jnp.float32)

    for copy in copies[3:7]:
        copy.wait()

    slots = lists.shape[1]
    entries = lists.shape[2]
    width = 3 + 2 * (LTR + 1)
    blocks = rows // 8
    for side, present in ((0, has_lower), (1, has_upper)):
        named = jnp.float32(0.0)
        for k in range(entries):
            chosen = lists[pair, 0, k]
            hit = chosen < slots if side == 0 else chosen >= 2 * slots
            named = named + jnp.where(hit, 1.0, 0.0)
        scale = named / entries
        base = side * width

        def oper_step(i, carry):
            other = i // blocks
            start = (x + other) % 2 * rows + other * dh * lt + i % blocks * 8
            at = pl.ds(pl.multiple_of(start, 8), 8)
            along_x = polar[0, at] * azim[0:1]
            along_y = polar[0, at] * azim[1:2]
            along_z = polar[1, at] * jnp.ones_like(along_x)
            u = (
                series[pair, base] * along_x
                + series[pair, base + 1] * along_y
                + series[pair, base + 2] * along_z
            )
            now, nxt = jnp.ones_like(u), u
            real, imag = jnp.zeros_like(u), jnp.zeros_like(u)
            for degree in range(LTR + 1):
                real = real + series[pair, base + 3 + 2 * degree] * now
                imag = imag + series[pair, base + 4 + 2 * degree] * now
                now, nxt = nxt, (
                    ((2.0 * degree + 3.0) / (degree + 2.0)) * (u * nxt)
                    - ((degree + 1.0) / (degree + 2.0)) * now
                )
            oper[side, 0, at] = real * scale
            oper[side, 1, at] = imag * scale
            return carry

        lax.fori_loop(0, blocks + (lt // 8 if crossed else 0), oper_step, 0)

    for copy in copies[7:]:
        copy.wait()

    ph2[1] = ph2[1] * (2 * x - 1).astype(jnp.float32)
    if crossed:
        x_copy(0).wait_recv()
        z_start(0, 1)
        y_first().wait_recv()

        @pl.when(turned_order == 0)
        def _():
            z_start(plain, 2)

        for i in range(1, plain):
            z_start(i, 0)
    else:
        for i in range(plain):
            x_copy(i).wait_recv()
            z_start(i, 1)

    lanes = lax.broadcasted_iota(jnp.int32, (slab, lp), 1)
    odd_lane = lanes % 2 == 1
    late_lane = lanes % 4 >= 2

    def woven(planes):
        pairs = [jnp.where(odd_lane, planes[(k + 1) % 4], planes[k]) for k in range(4)]
        mixed = [jnp.where(late_lane, pairs[(2 - h) % 4], pairs[-h % 4]) for h in range(4)]
        return [mixed[h] if h == 0 else pltpu.roll(mixed[h], lp - h, 1) for h in range(4)]

    def first_level(unit, place):
        source = jnp.concatenate(
            [taken[side, unit, place].reshape(4 * lt, lp) for side in range(2)], axis=0
        )
        high, low = split(source)
        both = dot(jnp.concatenate([high, low], axis=1), c1[...])
        odd_high, odd_low = split(both[:, :lp] + both[:, lp:])
        high = jnp.concatenate([high, odd_high], axis=1)
        low = jnp.concatenate([low, odd_low], axis=1)
        done = []
        cosine, sine = ph1[0], ph1[1]
        for side in range(2):
            parts = []
            for k in range(4):
                at = slice((4 * side + k) * lt, (4 * side + k + 1) * lt)
                parts.append(
                    dot(r1[...], jnp.concatenate([high[at], low[at], high[at]], axis=0))
                )
            sr, si, dre, dim = parts
            done.append((cosine * sr - sine * dim, cosine * si + sine * dre))
        return done

    def keep_own(unit):
        for side, (real, imag) in enumerate(first_level(unit, x)):
            first[side, 0] = real
            first[side, 1] = imag

    def unit_at(step):
        if not crossed:
            return 0, step
        kind = 1 - (step + turned_order * (step // 2)) % 2
        return kind, kind * (plain + (dh + step // 2) % 2) + (1 - kind) * (step // 2)

    def slab_at(kind, s):
        if not crossed:
            return box, s, x * rows + s * slab
        top = s // half_n
        low = s % half_n
        to_box = kind * (pair * 2 + top) + (1 - kind) * box
        to_dir = kind * (dh * half_n + low) + (1 - kind) * s
        row = kind * (top * rows + dh * lt + low * slab) + (1 - kind) * (x * rows + s * slab)
        return to_box, to_dir, row

    def slab_number(kind, o):
        if n_dir % 2:
            return (me + 1 + o) % n_dir
        top = kind * x + (1 - kind) * dh
        return (top + 1 - o // half_n) % 2 * half_n + (dl + 1 + o) % half_n

    def whose(kind, unit):
        if not crossed:
            return me * count + unit
        source = (unit - plain) * half_n + dl
        return kind * (source * count + plain + x) + (1 - kind) * (me * count + unit)

    def d_copy(kind, unit, o):
        s = slab_number(kind, o)
        to_box, to_dir, _ = slab_at(kind, s)
        rhs = whose(kind, unit)
        return pltpu.make_async_remote_copy(
            ready.at[unit, s], out.at[rhs], ds.at[unit, o], dr.at[rhs],
            (to_box, to_dir), device_id_type=MESH,
        )

    def do_unit(kind, unit):
        for side, (br, bi) in enumerate(first_level(unit, 1 - x)):
            ar, ai = first[side, 0], first[side, 1]
            for k, value in enumerate((ar + br, ai + bi, ar - br, ai - bi)):
                high, low = split(value)
                wide = dot(r2[kind], jnp.concatenate([high, low, high], axis=0))
                even[side, k] = wide
                high, low = split(wide)
                lhs2[side, k, :, : 2 * lp] = high
                lhs2[side, k, :, 2 * lp :] = low
        for o in range(n_dir):
            s = slab_number(kind, o)
            at = pl.ds(pl.multiple_of(s * slab, slab), slab)
            both = jnp.concatenate(
                [lhs2[side, k, at, :] for side in range(2) for k in range(4)], axis=0
            )
            odd = dot(jnp.concatenate([both, both[:, : 2 * lp]], axis=1), c2[...])
            row = pl.ds(pl.multiple_of(slab_at(kind, s)[2], slab), slab)
            planes = []
            for v in range(4):
                cut = slice(v * lp, (v + 1) * lp)
                cosine, sine = ph2[0, row, cut], ph2[1, row, cut]
                total = None
                for side in range(2):
                    if v < 2:
                        sr, si, dre, dim = [even[side, k, at, cut] for k in range(4)]
                    else:
                        sr, si, dre, dim = [
                            odd[(4 * side + k) * slab : (4 * side + k + 1) * slab,
                                (v - 2) * lp : (v - 1) * lp]
                            for k in range(4)
                        ]
                    gr = cosine * sr - sine * dim
                    gi = cosine * si + sine * dre
                    pr, pi = oper[side, 0, row, cut], oper[side, 1, row, cut]
                    real, imag = pr * gr - pi * gi, pr * gi + pi * gr
                    total = (real, imag) if total is None else (total[0] + real, total[1] + imag)
                planes.append(total)
            for c in range(2):
                parts = woven([planes[v][c] for v in (0, 2, 1, 3)])
                for h in range(4):
                    ready[unit, s, c, :, h * lp : (h + 1) * lp] = parts[h]
            if o == half_n - 1:
                for sent in range(half_n):
                    d_copy(kind, unit, sent).start()
            if o == n_dir - 1:
                for sent in range(half_n, n_dir - 1):
                    d_copy(kind, unit, sent).start()
                out[whose(kind, unit)] = ready[unit, s]

    def level_step(step, carry):
        kind, unit = unit_at(step)
        if crossed:
            @pl.when(step == 0)
            def _():
                y_start()

            @pl.when(step == 1)
            def _():
                for i in range(1, plain):
                    x_copy(i).wait_recv()
                    z_start(i, 1)

                @pl.when(turned_order == 1)
                def _():
                    z_start(plain, 2)

        for side, present in ((0, has_lower), (1, has_upper)):
            @pl.when(jnp.logical_and(present, step >= crossed))
            def _():
                arrived(side, unit, 1 - x)

        do_unit(kind, unit)

        @pl.when(step < count - 1)
        def _():
            _, following = unit_at(step + 1)
            for side, present in ((0, has_lower), (1, has_upper)):
                @pl.when(present)
                def _():
                    arrived(side, following, x)

            keep_own(following)

        return carry

    _, beginning = unit_at(0)
    for side, present in ((0, has_lower), (1, has_upper)):
        @pl.when(present)
        def _():
            arrived(side, beginning, x)

    keep_own(beginning)
    lax.fori_loop(0, count, level_step, 0)

    def out_arrived(rhs):
        pltpu.make_async_remote_copy(
            ready.at[0, 0], out.at[rhs], ds.at[0, 0], dr.at[rhs],
            (box, across), device_id_type=MESH,
        ).wait_recv()

    for step in range(count):
        kind, unit = unit_at(step)
        for o in range(n_dir - 1):
            d_copy(kind, unit, o).wait_send()
    for o in range(1, n_dir):
        for r in range(plain):
            out_arrived((me + o) % n_dir * count + r)
        if crossed:
            s = (x * half_n + dl + o) % n_dir
            for k in range(2):
                out_arrived((k * half_n + s % half_n) * count + plain + s // half_n)
    for i in range(plain):
        x_copy(i).wait_send()
    if crossed:
        y_first().wait_send()
    for side, sends, gets in ((0, has_upper, has_lower), (1, has_lower, has_upper)):
        @pl.when(sends)
        def _():
            for i in range(plain + crossed):
                for passed in range(3 if i == plain else 2):
                    z_copy(i, passed, side).wait_send()

        if crossed:
            @pl.when(gets)
            def _():
                y_copy(side).wait_send()


def per_device(n_box, n_dir, leaf_patterns, occupancy, pair_lists):
    _, count, _, lt, lp = leaf_patterns.shape
    assert leaf_patterns.shape[0] == 2
    slab = 2 * lt // n_dir
    crossed = int(count == 4 and n_dir % 2 == 0)
    steps = count - crossed
    bf16 = jnp.bfloat16
    lane = np.arange(lp)
    order = []
    for s in range(4):
        h = (lane % 4 - s) % 4
        order.append(lp * h + (lane - h) % lp)
    turn = (order[0] // 4).astype(np.int32)[None]
    first_order = np.concatenate([order[0], order[2]]) // 2
    second_odd = np.concatenate([order[1], order[3]])
    second_order = np.concatenate([order[0], order[2], second_odd])
    high, low = halves(interp_table(lp, 0.0)[first_order[lp:]][:, turn[0]].T)
    c1 = np.concatenate([np.concatenate([high, low], axis=1)] * 2, axis=0)
    row_high, row_low = halves(interp_table(lt, 0.5))
    r1 = np.concatenate([row_high, row_high, row_low], axis=1)
    row_high, row_low = halves(interp_table(2 * lt, 0.5))
    r2 = np.concatenate([row_high, row_high, row_low], axis=1)
    high, low = halves(interp_table(2 * lp, 0.0)[second_odd][:, first_order].T)
    c2 = np.concatenate([high, high, low], axis=0)
    st, _, cp, _ = sines(2 * lt, 2 * lp)
    angle = phase_first * st[:, None] * cp[first_order][None]
    ph1 = np.stack([np.cos(angle), np.sin(angle)]).astype(np.float32)
    st, ct, cp, sp = sines(4 * lt, 4 * lp)
    cp, sp = cp[second_order], sp[second_order]
    angle = phase_second * st[:, None] * sp[None]
    ph2 = np.stack([np.cos(angle), np.sin(angle)]).astype(np.float32)
    polar = np.stack([st, ct])[:, :, None].astype(np.float32)
    azim = np.stack([cp, sp]).astype(np.float32)
    series = series_table(n_box // 2)
    operands = (
        leaf_patterns, occupancy, pair_lists, series, c1, r1, r2, c2, ph1, ph2, polar, azim,
        turn,
    )
    chunk = (2, slab, 4 * lp)
    f32 = jnp.float32
    rows = 2 * lt
    result = pl.pallas_call(
        functools.partial(kernel, (n_box, n_dir, count, lt, lp, slab, crossed)),
        out_shape=jax.ShapeDtypeStruct((n_dir * count,) + chunk, f32),
        in_specs=[pl.BlockSpec(memory_space=pltpu.HBM)] * len(operands),
        out_specs=pl.BlockSpec(memory_space=pltpu.VMEM),
        scratch_shapes=[
            pltpu.VMEM(leaf_patterns.shape, f32),
            pltpu.SMEM(occupancy.shape, jnp.int32),
            pltpu.SMEM(pair_lists.shape, jnp.int32),
            pltpu.SMEM(series.shape, f32),
            pltpu.VMEM(c1.shape, bf16),
            pltpu.VMEM(r1.shape, bf16),
            pltpu.VMEM((1 + crossed, rows) + r2.shape[1:], bf16),
            pltpu.VMEM(c2.shape, bf16),
            pltpu.VMEM(ph1.shape, f32),
            pltpu.VMEM(ph2.shape, f32),
            pltpu.VMEM(polar.shape, f32),
            pltpu.VMEM(azim.shape, f32),
            pltpu.VMEM(turn.shape, jnp.int32),
            pltpu.VMEM((count, 4, lt, lp), f32),
            pltpu.VMEM((steps, 4, lt, lp), f32),
            pltpu.VMEM((4, lt, lp), f32),
            pltpu.VMEM((2, count, 2, 4, lt, lp), f32),
            pltpu.VMEM((2, 2, rows, 2 * lp), f32),
            pltpu.VMEM((2, 4, rows, 4 * lp), bf16),
            pltpu.VMEM((2, 4, rows, 2 * lp), f32),
            pltpu.VMEM((count, n_dir) + chunk, f32),
            pltpu.VMEM((2, 2, 2 * rows, 4 * lp), f32),
            pltpu.SemaphoreType.DMA((len(operands) + 2 * crossed,)),
            pltpu.SemaphoreType.DMA((steps,)),
            pltpu.SemaphoreType.DMA((steps,)),
            pltpu.SemaphoreType.DMA((2, count, 3)),
            pltpu.SemaphoreType.DMA((2, count, 2)),
            pltpu.SemaphoreType.DMA((4,)),
            pltpu.SemaphoreType.DMA((count, n_dir)),
            pltpu.SemaphoreType.DMA((n_dir * count,)),
        ],
        compiler_params=pltpu.CompilerParams(
            collective_id=0, has_side_effects=True, vmem_limit_bytes=48 << 20
        ),
    )(*[pltpu.with_memory_space_constraint(jnp.asarray(operand), pltpu.HBM) for operand in operands])
    return result.reshape(1, 1, n_dir * count, *chunk)


def solution(mesh):
    placed = (P("box", "dir", None, None, None), P("box"), P())
    return jax.shard_map(
        functools.partial(per_device, mesh.shape["box"], mesh.shape["dir"]),
        mesh=mesh,
        in_specs=placed,
        out_specs=P("box", None, None, None, "dir", None),
        check_vma=False,
    )
```

```python
import functools

import jax
import jax.numpy as jnp
import numpy as np
from jax import lax
from jax.experimental import pallas as pl
from jax.experimental.pallas import tpu as pltpu
from jax.sharding import PartitionSpec as P

MESH = pl.DeviceIdType.MESH
LTR = 16
full_count = 16.0
phase_first = 16.0
phase_second = 64.0
translate_wave = 20.0


def interp_table(points, offset):
    orders = np.arange(points // 2 + 1, dtype=np.float64)
    weights = np.where((orders == 0) | (orders == points // 2), 1.0, 2.0) / points
    source = (np.arange(points) + offset) / points
    target = (np.arange(2 * points) + offset) / (2 * points)
    angle = 2.0 * np.pi * (target[:, None, None] - source[None, :, None]) * orders
    return (np.cos(angle) * weights).sum(-1)


def halves(table):
    high = np.asarray(table, np.float32).astype(jnp.bfloat16)
    low = (np.asarray(table, np.float64) - high.astype(np.float64)).astype(jnp.bfloat16)
    return high, low


def sines(rows, columns):
    theta = np.pi * (np.arange(rows) + 0.5) / rows
    phi = 2.0 * np.pi * np.arange(columns) / columns
    return np.sin(theta), np.cos(theta), np.cos(phi), np.sin(phi)


def center(g):
    return np.array([g % 4, g // 4 % 4, g // 16], np.float64)


def series_table(pairs):
    table = np.zeros((pairs, 2 * (3 + 2 * (LTR + 1))), np.float64)
    width = 3 + 2 * (LTR + 1)
    for g in range(pairs):
        for side, s in enumerate((g - 1, g + 1)):
            if not 0 <= s < pairs:
                continue
            r = center(g) - center(s)
            distance = np.sqrt((r * r).sum())
            x = translate_wave * distance
            now = (np.sin(x) - 1j * np.cos(x)) / x
            nxt = ((np.sin(x) - x * np.cos(x)) - 1j * (x * np.sin(x) + np.cos(x))) / x**2
            table[g, side * width : side * width + 3] = r / distance
            for degree in range(LTR + 1):
                value = (1j**degree) * (2 * degree + 1) * now
                table[g, side * width + 3 + 2 * degree] = value.real
                table[g, side * width + 4 + 2 * degree] = value.imag
                now, nxt = nxt, (2 * degree + 3) / x * nxt - now
    return table.astype(np.float32)


def split(value):
    high = value.astype(jnp.bfloat16)
    low = (value - high.astype(jnp.float32)).astype(jnp.bfloat16)
    return high, low


def dot(a, b):
    return jnp.dot(a, b, preferred_element_type=jnp.float32)


def kernel(
    sizes,
    leaf_in, occ_in, lists_in, series_in, c1_in, r1_in, r2_in, c2_in, ph1_in, ph2_in,
    polar_in, azim_in, turn_in,
    out,
    leaf, occ, lists, series, c1, r1, r2, c2, ph1, ph2, polar, azim, turn,
    mine, gath, yours, taken, first, lhs2, even, ready, oper,
    loads, xs, xr, ls, lr, ys, ds, dr,
):
    n_box, n_dir, count, lt, lp, slab, crossed = sizes
    plain = count - 2 * crossed
    half_n = n_dir // 2
    rows = 2 * lt
    box = lax.axis_index("box")
    me = lax.axis_index("dir")
    x = box % 2
    pair = box // 2
    dh = me // half_n
    dl = me % half_n
    turned_order = (dl + 1) % 2
    has_lower = pair > 0
    has_upper = pair < n_box // 2 - 1
    partner = box + 1 - 2 * x
    across = (me + half_n) % n_dir

    barrier = pltpu.get_barrier_semaphore()
    for o in range(1, n_dir):
        pl.semaphore_signal(
            barrier, inc=1, device_id=(box, (me + o) % n_dir), device_id_type=MESH
        )
    if crossed:
        for k in range(half_n):
            pl.semaphore_signal(
                barrier, inc=1, device_id=(partner, dh * half_n + k), device_id_type=MESH
            )
        for present, by in ((has_lower, -2), (has_upper, 2)):
            @pl.when(present)
            def _():
                pl.semaphore_signal(
                    barrier, inc=1, device_id=(partner + by, me), device_id_type=MESH
                )
    else:
        pl.semaphore_signal(barrier, inc=1, device_id=(partner, me), device_id_type=MESH)
    for present, by in ((has_lower, -2), (has_upper, 2)):
        @pl.when(present)
        def _():
            pl.semaphore_signal(barrier, inc=1, device_id=(box + by, me), device_id_type=MESH)

    start_own = pl.multiple_of(x * rows, rows)
    pairs_in = [
        (leaf_in, leaf), (occ_in, occ), (turn_in, turn), (lists_in, lists), (series_in, series),
        (polar_in, polar), (azim_in, azim), (c1_in, c1), (r1_in, r1),
        (ph1_in, ph1), (c2_in, c2), (ph2_in, ph2),
        (r2_in.at[pl.ds(start_own, rows)], r2.at[0]),
    ]
    if crossed:
        for k in range(2):
            start = pl.multiple_of(k * rows + dh * lt, lt)
            pairs_in.append((r2_in.at[pl.ds(start, lt)], r2.at[1, pl.ds(k * lt, lt)]))
    copies = [
        pltpu.make_async_copy(source, target, loads.at[i])
        for i, (source, target) in enumerate(pairs_in)
    ]
    for copy in copies:
        copy.start()
    for copy in copies[:3]:
        copy.wait()

    w0 = occ[0].astype(jnp.float32) / full_count
    w1 = occ[1].astype(jnp.float32) / full_count
    turned = jnp.broadcast_to(turn[...], (lt, lp))
    for r in range(count):
        for c in range(2):
            a = jnp.take_along_axis(leaf[0, r, c], turned, axis=1) * w0
            b = jnp.take_along_axis(leaf[1, r, c], turned, axis=1) * w1
            mine[r, c] = a + b
            mine[r, 2 + c] = b - a

    pl.semaphore_wait(
        barrier,
        n_dir - 1 + (half_n if crossed else 1)
        + (1 + crossed) * (has_lower.astype(jnp.int32) + has_upper.astype(jnp.int32)),
    )

    def x_copy(i):
        return pltpu.make_async_remote_copy(
            mine.at[i], gath.at[i], xs.at[i], xr.at[i], (partner, me), device_id_type=MESH
        )

    def z_copy(i, passed, side):
        by = 2 - 4 * side
        target = box + by
        if i == plain:
            unit = plain + dh
            source, place = mine.at[plain + x], x
            if passed == 1:
                source, target = mine.at[plain + 1 - x], partner + by
            elif passed == 2:
                source, unit = yours, plain + 1 - dh
        else:
            unit = i
            source, place = (gath.at[i], 1 - x) if passed else (mine.at[i], x)
        return pltpu.make_async_remote_copy(
            source, taken.at[side, unit, place], ls.at[side, i, passed],
            lr.at[side, unit, place], (target, me), device_id_type=MESH,
        )

    def z_start(i, passed):
        @pl.when(has_upper)
        def _():
            z_copy(i, passed, 0).start()

        @pl.when(has_lower)
        def _():
            z_copy(i, passed, 1).start()

    def arrived(side, unit, place):
        pltpu.make_async_remote_copy(
            mine.at[0], taken.at[side, unit, place], ls.at[side, 0, 0],
            lr.at[side, unit, place], (partner, me), device_id_type=MESH,
        ).wait_recv()

    def y_first():
        return pltpu.make_async_remote_copy(
            mine.at[plain + x], yours, ys.at[2], ys.at[3], (box, across),
            device_id_type=MESH,
        )

    def y_copy(side):
        block = taken.at[side, plain + dh, 1 - x]
        return pltpu.make_async_remote_copy(
            block, block, ys.at[side], lr.at[side, plain + dh, 1 - x],
            (box, across), device_id_type=MESH,
        )

    def y_start():
        for side, present in ((0, has_lower), (1, has_upper)):
            @pl.when(present)
            def _():
                arrived(side, plain + dh, 1 - x)
                y_copy(side).start()

    if crossed:
        y_first().start()
        x_copy(0).start()
        z_start(plain, 0)
        z_start(plain, 1)
        z_start(0, 0)
        for i in range(1, plain):
            x_copy(i).start()
    else:
        for i in range(plain):
            x_copy(i).start()
            z_start(i, 0)

    for side, present in ((0, has_lower), (1, has_upper)):
        @pl.when(jnp.logical_not(present))
        def _():
            taken[side] = jnp.zeros(taken.shape[1:], jnp.float32)

    for copy in copies[3:7]:
        copy.wait()

    slots = lists.shape[1]
    entries = lists.shape[2]
    width = 3 + 2 * (LTR + 1)
    blocks = rows // 8
    for side, present in ((0, has_lower), (1, has_upper)):
        named = jnp.float32(0.0)
        for k in range(entries):
            chosen = lists[pair, 0, k]
            hit = chosen < slots if side == 0 else chosen >= 2 * slots
            named = named + jnp.where(hit, 1.0, 0.0)
        scale = named / entries
        base = side * width

        def oper_step(i, carry):
            other = i // blocks
            start = (x + other) % 2 * rows + other * dh * lt + i % blocks * 8
            at = pl.ds(pl.multiple_of(start, 8), 8)
            along_x = polar[0, at] * azim[0:1]
            along_y = polar[0, at] * azim[1:2]
            along_z = polar[1, at] * jnp.ones_like(along_x)
            u = (
                series[pair, base] * along_x
                + series[pair, base + 1] * along_y
                + series[pair, base + 2] * along_z
            )
            now, nxt = jnp.ones_like(u), u
            real, imag = jnp.zeros_like(u), jnp.zeros_like(u)
            for degree in range(LTR + 1):
                real = real + series[pair, base + 3 + 2 * degree] * now
                imag = imag + series[pair, base + 4 + 2 * degree] * now
                now, nxt = nxt, (
                    ((2.0 * degree + 3.0) / (degree + 2.0)) * (u * nxt)
                    - ((degree + 1.0) / (degree + 2.0)) * now
                )
            oper[side, 0, at] = real * scale
            oper[side, 1, at] = imag * scale
            return carry

        lax.fori_loop(0, blocks + (lt // 8 if crossed else 0), oper_step, 0)

    for copy in copies[7:]:
        copy.wait()

    ph2[1] = ph2[1] * (2 * x - 1).astype(jnp.float32)
    if crossed:
        x_copy(0).wait_recv()
        z_start(0, 1)
        y_first().wait_recv()

        @pl.when(turned_order == 0)
        def _():
            z_start(plain, 2)

        for i in range(1, plain):
            z_start(i, 0)
    else:
        for i in range(plain):
            x_copy(i).wait_recv()
            z_start(i, 1)

    lanes = lax.broadcasted_iota(jnp.int32, (slab, lp), 1)
    odd_lane = lanes % 2 == 1
    late_lane = lanes % 4 >= 2

    def woven(planes):
        pairs = [jnp.where(odd_lane, planes[(k + 1) % 4], planes[k]) for k in range(4)]
        mixed = [jnp.where(late_lane, pairs[(2 - h) % 4], pairs[-h % 4]) for h in range(4)]
        return [mixed[h] if h == 0 else pltpu.roll(mixed[h], lp - h, 1) for h in range(4)]

    def first_level(unit, place):
        source = jnp.concatenate(
            [taken[side, unit, place].reshape(4 * lt, lp) for side in range(2)], axis=0
        )
        high, low = split(source)
        both = dot(jnp.concatenate([high, low], axis=1), c1[...])
        odd_high, odd_low = split(both[:, :lp] + both[:, lp:])
        high = jnp.concatenate([high, odd_high], axis=1)
        low = jnp.concatenate([low, odd_low], axis=1)
        done = []
        cosine, sine = ph1[0], ph1[1]
        for side in range(2):
            parts = []
            for k in range(4):
                at = slice((4 * side + k) * lt, (4 * side + k + 1) * lt)
                parts.append(
                    dot(r1[...], jnp.concatenate([high[at], low[at], high[at]], axis=0))
                )
            sr, si, dre, dim = parts
            done.append((cosine * sr - sine * dim, cosine * si + sine * dre))
        return done

    def keep_own(unit):
        for side, (real, imag) in enumerate(first_level(unit, x)):
            first[side, 0] = real
            first[side, 1] = imag

    def unit_at(step):
        if not crossed:
            return 0, step
        kind = 1 - (step + turned_order * (step // 2)) % 2
        return kind, kind * (plain + (dh + step // 2) % 2) + (1 - kind) * (step // 2)

    def slab_at(kind, s):
        if not crossed:
            return box, s, x * rows + s * slab
        top = s // half_n
        low = s % half_n
        to_box = kind * (pair * 2 + top) + (1 - kind) * box
        to_dir = kind * (dh * half_n + low) + (1 - kind) * s
        row = kind * (top * rows + dh * lt + low * slab) + (1 - kind) * (x * rows + s * slab)
        return to_box, to_dir, row

    def slab_number(kind, o):
        if n_dir % 2:
            return (me + 1 + o) % n_dir
        top = kind * x + (1 - kind) * dh
        return (top + 1 - o // half_n) % 2 * half_n + (dl + 1 + o) % half_n

    def whose(kind, unit):
        if not crossed:
            return me * count + unit
        source = (unit - plain) * half_n + dl
        return kind * (source * count + plain + x) + (1 - kind) * (me * count + unit)

    def d_copy(kind, unit, o):
        s = slab_number(kind, o)
        to_box, to_dir, _ = slab_at(kind, s)
        rhs = whose(kind, unit)
        return pltpu.make_async_remote_copy(
            ready.at[unit, s], out.at[rhs], ds.at[unit, o], dr.at[rhs],
            (to_box, to_dir), device_id_type=MESH,
        )

    def do_unit(kind, unit):
        for side, (br, bi) in enumerate(first_level(unit, 1 - x)):
            ar, ai = first[side, 0], first[side, 1]
            for k, value in enumerate((ar + br, ai + bi, ar - br, ai - bi)):
                high, low = split(value)
                wide = dot(r2[kind], jnp.concatenate([high, low, high], axis=0))
                even[side, k] = wide
                high, low = split(wide)
                lhs2[side, k, :, : 2 * lp] = high
                lhs2[side, k, :, 2 * lp :] = low
        for o in range(n_dir):
            s = slab_number(kind, o)
            at = pl.ds(pl.multiple_of(s * slab, slab), slab)
            both = jnp.concatenate(
                [lhs2[side, k, at, :] for side in range(2) for k in range(4)], axis=0
            )
            odd = dot(jnp.concatenate([both, both[:, : 2 * lp]], axis=1), c2[...])
            row = pl.ds(pl.multiple_of(slab_at(kind, s)[2], slab), slab)
            planes = []
            for v in range(4):
                cut = slice(v * lp, (v + 1) * lp)
                cosine, sine = ph2[0, row, cut], ph2[1, row, cut]
                total = None
                for side in range(2):
                    if v < 2:
                        sr, si, dre, dim = [even[side, k, at, cut] for k in range(4)]
                    else:
                        sr, si, dre, dim = [
                            odd[(4 * side + k) * slab : (4 * side + k + 1) * slab,
                                (v - 2) * lp : (v - 1) * lp]
                            for k in range(4)
                        ]
                    gr = cosine * sr - sine * dim
                    gi = cosine * si + sine * dre
                    pr, pi = oper[side, 0, row, cut], oper[side, 1, row, cut]
                    real, imag = pr * gr - pi * gi, pr * gi + pi * gr
                    total = (real, imag) if total is None else (total[0] + real, total[1] + imag)
                planes.append(total)
            for c in range(2):
                parts = woven([planes[v][c] for v in (0, 2, 1, 3)])
                for h in range(4):
                    ready[unit, s, c, :, h * lp : (h + 1) * lp] = parts[h]
            if o == half_n - 1:
                for sent in range(half_n):
                    d_copy(kind, unit, sent).start()
            if o == n_dir - 1:
                for sent in range(half_n, n_dir - 1):
                    d_copy(kind, unit, sent).start()
                out[whose(kind, unit)] = ready[unit, s]

    def level_step(step, carry):
        kind, unit = unit_at(step)
        if crossed:
            @pl.when(step == 0)
            def _():
                y_start()

            @pl.when(step == 2 - turned_order)
            def _():
                for i in range(1, plain):
                    x_copy(i).wait_recv()
                    z_start(i, 1)

                @pl.when(turned_order == 1)
                def _():
                    z_start(plain, 2)

        for side, present in ((0, has_lower), (1, has_upper)):
            @pl.when(jnp.logical_and(present, step >= crossed))
            def _():
                arrived(side, unit, 1 - x)

        do_unit(kind, unit)

        @pl.when(step < count - 1)
        def _():
            _, following = unit_at(step + 1)
            for side, present in ((0, has_lower), (1, has_upper)):
                @pl.when(present)
                def _():
                    arrived(side, following, x)

            keep_own(following)

        return carry

    _, beginning = unit_at(0)
    for side, present in ((0, has_lower), (1, has_upper)):
        @pl.when(present)
        def _():
            arrived(side, beginning, x)

    keep_own(beginning)
    lax.fori_loop(0, count, level_step, 0)

    def out_arrived(rhs):
        pltpu.make_async_remote_copy(
            ready.at[0, 0], out.at[rhs], ds.at[0, 0], dr.at[rhs],
            (box, across), device_id_type=MESH,
        ).wait_recv()

    for step in range(count):
        kind, unit = unit_at(step)
        for o in range(n_dir - 1):
            d_copy(kind, unit, o).wait_send()
    for o in range(1, n_dir):
        for r in range(plain):
            out_arrived((me + o) % n_dir * count + r)
        if crossed:
            s = (x * half_n + dl + o) % n_dir
            for k in range(2):
                out_arrived((k * half_n + s % half_n) * count + plain + s // half_n)
    for i in range(plain):
        x_copy(i).wait_send()
    if crossed:
        y_first().wait_send()
    for side, sends, gets in ((0, has_upper, has_lower), (1, has_lower, has_upper)):
        @pl.when(sends)
        def _():
            for i in range(plain + crossed):
                for passed in range(3 if i == plain else 2):
                    z_copy(i, passed, side).wait_send()

        if crossed:
            @pl.when(gets)
            def _():
                y_copy(side).wait_send()


def per_device(n_box, n_dir, leaf_patterns, occupancy, pair_lists):
    _, count, _, lt, lp = leaf_patterns.shape
    assert leaf_patterns.shape[0] == 2
    slab = 2 * lt // n_dir
    crossed = int(count == 4 and n_dir % 2 == 0)
    steps = count - crossed
    bf16 = jnp.bfloat16
    lane = np.arange(lp)
    order = []
    for s in range(4):
        h = (lane % 4 - s) % 4
        order.append(lp * h + (lane - h) % lp)
    turn = (order[0] // 4).astype(np.int32)[None]
    first_order = np.concatenate([order[0], order[2]]) // 2
    second_odd = np.concatenate([order[1], order[3]])
    second_order = np.concatenate([order[0], order[2], second_odd])
    high, low = halves(interp_table(lp, 0.0)[first_order[lp:]][:, turn[0]].T)
    c1 = np.concatenate([np.concatenate([high, low], axis=1)] * 2, axis=0)
    row_high, row_low = halves(interp_table(lt, 0.5))
    r1 = np.concatenate([row_high, row_high, row_low], axis=1)
    row_high, row_low = halves(interp_table(2 * lt, 0.5))
    r2 = np.concatenate([row_high, row_high, row_low], axis=1)
    high, low = halves(interp_table(2 * lp, 0.0)[second_odd][:, first_order].T)
    c2 = np.concatenate([high, high, low], axis=0)
    st, _, cp, _ = sines(2 * lt, 2 * lp)
    angle = phase_first * st[:, None] * cp[first_order][None]
    ph1 = np.stack([np.cos(angle), np.sin(angle)]).astype(np.float32)
    st, ct, cp, sp = sines(4 * lt, 4 * lp)
    cp, sp = cp[second_order], sp[second_order]
    angle = phase_second * st[:, None] * sp[None]
    ph2 = np.stack([np.cos(angle), np.sin(angle)]).astype(np.float32)
    polar = np.stack([st, ct])[:, :, None].astype(np.float32)
    azim = np.stack([cp, sp]).astype(np.float32)
    series = series_table(n_box // 2)
    operands = (
        leaf_patterns, occupancy, pair_lists, series, c1, r1, r2, c2, ph1, ph2, polar, azim,
        turn,
    )
    chunk = (2, slab, 4 * lp)
    f32 = jnp.float32
    rows = 2 * lt
    result = pl.pallas_call(
        functools.partial(kernel, (n_box, n_dir, count, lt, lp, slab, crossed)),
        out_shape=jax.ShapeDtypeStruct((n_dir * count,) + chunk, f32),
        in_specs=[pl.BlockSpec(memory_space=pltpu.HBM)] * len(operands),
        out_specs=pl.BlockSpec(memory_space=pltpu.VMEM),
        scratch_shapes=[
            pltpu.VMEM(leaf_patterns.shape, f32),
            pltpu.SMEM(occupancy.shape, jnp.int32),
            pltpu.SMEM(pair_lists.shape, jnp.int32),
            pltpu.SMEM(series.shape, f32),
            pltpu.VMEM(c1.shape, bf16),
            pltpu.VMEM(r1.shape, bf16),
            pltpu.VMEM((1 + crossed, rows) + r2.shape[1:], bf16),
            pltpu.VMEM(c2.shape, bf16),
            pltpu.VMEM(ph1.shape, f32),
            pltpu.VMEM(ph2.shape, f32),
            pltpu.VMEM(polar.shape, f32),
            pltpu.VMEM(azim.shape, f32),
            pltpu.VMEM(turn.shape, jnp.int32),
            pltpu.VMEM((count, 4, lt, lp), f32),
            pltpu.VMEM((steps, 4, lt, lp), f32),
            pltpu.VMEM((4, lt, lp), f32),
            pltpu.VMEM((2, count, 2, 4, lt, lp), f32),
            pltpu.VMEM((2, 2, rows, 2 * lp), f32),
            pltpu.VMEM((2, 4, rows, 4 * lp), bf16),
            pltpu.VMEM((2, 4, rows, 2 * lp), f32),
            pltpu.VMEM((count, n_dir) + chunk, f32),
            pltpu.VMEM((2, 2, 2 * rows, 4 * lp), f32),
            pltpu.SemaphoreType.DMA((len(operands) + 2 * crossed,)),
            pltpu.SemaphoreType.DMA((steps,)),
            pltpu.SemaphoreType.DMA((steps,)),
            pltpu.SemaphoreType.DMA((2, count, 3)),
            pltpu.SemaphoreType.DMA((2, count, 2)),
            pltpu.SemaphoreType.DMA((4,)),
            pltpu.SemaphoreType.DMA((count, n_dir)),
            pltpu.SemaphoreType.DMA((n_dir * count,)),
        ],
        compiler_params=pltpu.CompilerParams(
            collective_id=0, has_side_effects=True, vmem_limit_bytes=48 << 20
        ),
    )(*[pltpu.with_memory_space_constraint(jnp.asarray(operand), pltpu.HBM) for operand in operands])
    return result.reshape(1, 1, n_dir * count, *chunk)


def solution(mesh):
    placed = (P("box", "dir", None, None, None), P("box"), P())
    return jax.shard_map(
        functools.partial(per_device, mesh.shape["box"], mesh.shape["dir"]),
        mesh=mesh,
        in_specs=placed,
        out_specs=P("box", None, None, None, "dir", None),
        check_vma=False,
    )
```

```python
import functools

import jax
import jax.numpy as jnp
import numpy as np
from jax import lax
from jax.experimental import pallas as pl
from jax.experimental.pallas import tpu as pltpu
from jax.sharding import PartitionSpec as P

MESH = pl.DeviceIdType.MESH
LTR = 16
full_count = 16.0
phase_first = 16.0
phase_second = 64.0
translate_wave = 20.0


def interp_table(points, offset):
    orders = np.arange(points // 2 + 1, dtype=np.float64)
    weights = np.where((orders == 0) | (orders == points // 2), 1.0, 2.0) / points
    source = (np.arange(points) + offset) / points
    target = (np.arange(2 * points) + offset) / (2 * points)
    angle = 2.0 * np.pi * (target[:, None, None] - source[None, :, None]) * orders
    return (np.cos(angle) * weights).sum(-1)


def halves(table):
    high = np.asarray(table, np.float32).astype(jnp.bfloat16)
    low = (np.asarray(table, np.float64) - high.astype(np.float64)).astype(jnp.bfloat16)
    return high, low


def sines(rows, columns):
    theta = np.pi * (np.arange(rows) + 0.5) / rows
    phi = 2.0 * np.pi * np.arange(columns) / columns
    return np.sin(theta), np.cos(theta), np.cos(phi), np.sin(phi)


def center(g):
    return np.array([g % 4, g // 4 % 4, g // 16], np.float64)


def series_table(pairs):
    table = np.zeros((pairs, 2 * (3 + 2 * (LTR + 1))), np.float64)
    width = 3 + 2 * (LTR + 1)
    for g in range(pairs):
        for side, s in enumerate((g - 1, g + 1)):
            if not 0 <= s < pairs:
                continue
            r = center(g) - center(s)
            distance = np.sqrt((r * r).sum())
            x = translate_wave * distance
            now = (np.sin(x) - 1j * np.cos(x)) / x
            nxt = ((np.sin(x) - x * np.cos(x)) - 1j * (x * np.sin(x) + np.cos(x))) / x**2
            table[g, side * width : side * width + 3] = r / distance
            for degree in range(LTR + 1):
                value = (1j**degree) * (2 * degree + 1) * now
                table[g, side * width + 3 + 2 * degree] = value.real
                table[g, side * width + 4 + 2 * degree] = value.imag
                now, nxt = nxt, (2 * degree + 3) / x * nxt - now
    return table.astype(np.float32)


def split(value):
    high = value.astype(jnp.bfloat16)
    low = (value - high.astype(jnp.float32)).astype(jnp.bfloat16)
    return high, low


def dot(a, b):
    return jnp.dot(a, b, preferred_element_type=jnp.float32)


def kernel(
    sizes,
    leaf_in, occ_in, lists_in, series_in, c1_in, r1_in, r2_in, c2_in, ph1_in, ph2_in,
    polar_in, azim_in, turn_in,
    out,
    leaf, occ, lists, series, c1, r1, r2, c2, ph1, ph2, polar, azim, turn,
    mine, gath, yours, taken, first, lhs2, even, ready, oper,
    loads, xs, xr, ls, lr, ys, ds, dr,
):
    n_box, n_dir, count, lt, lp, slab, crossed = sizes
    plain = count - 2 * crossed
    half_n = n_dir // 2
    rows = 2 * lt
    box = lax.axis_index("box")
    me = lax.axis_index("dir")
    x = box % 2
    pair = box // 2
    dh = me // half_n
    dl = me % half_n
    turned_order = (dl + 1) % 2
    has_lower = pair > 0
    has_upper = pair < n_box // 2 - 1
    partner = box + 1 - 2 * x
    across = (me + half_n) % n_dir

    barrier = pltpu.get_barrier_semaphore()
    for o in range(1, n_dir):
        pl.semaphore_signal(
            barrier, inc=1, device_id=(box, (me + o) % n_dir), device_id_type=MESH
        )
    if crossed:
        for k in range(half_n):
            pl.semaphore_signal(
                barrier, inc=1, device_id=(partner, dh * half_n + k), device_id_type=MESH
            )
        for present, by in ((has_lower, -2), (has_upper, 2)):
            @pl.when(present)
            def _():
                pl.semaphore_signal(
                    barrier, inc=1, device_id=(partner + by, me), device_id_type=MESH
                )
    else:
        pl.semaphore_signal(barrier, inc=1, device_id=(partner, me), device_id_type=MESH)
    for present, by in ((has_lower, -2), (has_upper, 2)):
        @pl.when(present)
        def _():
            pl.semaphore_signal(barrier, inc=1, device_id=(box + by, me), device_id_type=MESH)

    start_own = pl.multiple_of(x * rows, rows)
    pairs_in = [
        (leaf_in, leaf), (occ_in, occ), (turn_in, turn), (lists_in, lists), (series_in, series),
        (polar_in, polar), (azim_in, azim), (c1_in, c1), (r1_in, r1),
        (ph1_in, ph1), (c2_in, c2), (ph2_in, ph2),
        (r2_in.at[pl.ds(start_own, rows)], r2.at[0]),
    ]
    if crossed:
        for k in range(2):
            start = pl.multiple_of(k * rows + dh * lt, lt)
            pairs_in.append((r2_in.at[pl.ds(start, lt)], r2.at[1, pl.ds(k * lt, lt)]))
    copies = [
        pltpu.make_async_copy(source, target, loads.at[i])
        for i, (source, target) in enumerate(pairs_in)
    ]
    for copy in copies:
        copy.start()
    for copy in copies[:3]:
        copy.wait()

    w0 = occ[0].astype(jnp.float32) / full_count
    w1 = occ[1].astype(jnp.float32) / full_count
    turned = jnp.broadcast_to(turn[...], (lt, lp))
    for r in range(count):
        for c in range(2):
            a = jnp.take_along_axis(leaf[0, r, c], turned, axis=1) * w0
            b = jnp.take_along_axis(leaf[1, r, c], turned, axis=1) * w1
            mine[r, c] = a + b
            mine[r, 2 + c] = b - a

    pl.semaphore_wait(
        barrier,
        n_dir - 1 + (half_n if crossed else 1)
        + (1 + crossed) * (has_lower.astype(jnp.int32) + has_upper.astype(jnp.int32)),
    )

    def x_copy(i):
        return pltpu.make_async_remote_copy(
            mine.at[i], gath.at[i], xs.at[i], xr.at[i], (partner, me), device_id_type=MESH
        )

    def z_copy(i, passed, side):
        by = 2 - 4 * side
        target = box + by
        if i == plain:
            unit = plain + dh
            source, place = mine.at[plain + x], x
            if passed == 1:
                source, target = mine.at[plain + 1 - x], partner + by
            elif passed == 2:
                source, unit = yours, plain + 1 - dh
        else:
            unit = i
            source, place = (gath.at[i], 1 - x) if passed else (mine.at[i], x)
        return pltpu.make_async_remote_copy(
            source, taken.at[side, unit, place], ls.at[side, i, passed],
            lr.at[side, unit, place], (target, me), device_id_type=MESH,
        )

    def z_start(i, passed):
        @pl.when(has_upper)
        def _():
            z_copy(i, passed, 0).start()

        @pl.when(has_lower)
        def _():
            z_copy(i, passed, 1).start()

    def arrived(side, unit, place):
        pltpu.make_async_remote_copy(
            mine.at[0], taken.at[side, unit, place], ls.at[side, 0, 0],
            lr.at[side, unit, place], (partner, me), device_id_type=MESH,
        ).wait_recv()

    def y_first():
        return pltpu.make_async_remote_copy(
            mine.at[plain + x], yours, ys.at[4], ys.at[5], (box, across),
            device_id_type=MESH,
        )

    def y_copy(side, place, sent):
        block = taken.at[side, plain + dh, place]
        return pltpu.make_async_remote_copy(
            block, block, ys.at[2 * sent + side], lr.at[side, plain + dh, place],
            (box, across), device_id_type=MESH,
        )

    def y_start():
        for side, present in ((0, has_lower), (1, has_upper)):
            @pl.when(present)
            def _():
                arrived(side, plain + dh, 1 - x)
                y_copy(side, 1 - x, 0).start()

    if crossed:
        @pl.when(turned_order == 0)
        def _():
            y_first().start()

        x_copy(0).start()
        z_start(plain, 0)
        z_start(plain, 1)
        z_start(0, 0)
        for i in range(1, plain):
            x_copy(i).start()

        @pl.when(turned_order == 0)
        def _():
            for i in range(1, plain):
                z_start(i, 0)

    else:
        for i in range(plain):
            x_copy(i).start()
            z_start(i, 0)

    for side, present in ((0, has_lower), (1, has_upper)):
        @pl.when(jnp.logical_not(present))
        def _():
            taken[side] = jnp.zeros(taken.shape[1:], jnp.float32)

    for copy in copies[3:7]:
        copy.wait()

    slots = lists.shape[1]
    entries = lists.shape[2]
    width = 3 + 2 * (LTR + 1)
    blocks = rows // 8
    for side, present in ((0, has_lower), (1, has_upper)):
        named = jnp.float32(0.0)
        for k in range(entries):
            chosen = lists[pair, 0, k]
            hit = chosen < slots if side == 0 else chosen >= 2 * slots
            named = named + jnp.where(hit, 1.0, 0.0)
        scale = named / entries
        base = side * width

        def oper_step(i, carry):
            other = i // blocks
            start = (x + other) % 2 * rows + other * dh * lt + i % blocks * 8
            at = pl.ds(pl.multiple_of(start, 8), 8)
            along_x = polar[0, at] * azim[0:1]
            along_y = polar[0, at] * azim[1:2]
            along_z = polar[1, at] * jnp.ones_like(along_x)
            u = (
                series[pair, base] * along_x
                + series[pair, base + 1] * along_y
                + series[pair, base + 2] * along_z
            )
            now, nxt = jnp.ones_like(u), u
            real, imag = jnp.zeros_like(u), jnp.zeros_like(u)
            for degree in range(LTR + 1):
                real = real + series[pair, base + 3 + 2 * degree] * now
                imag = imag + series[pair, base + 4 + 2 * degree] * now
                now, nxt = nxt, (
                    ((2.0 * degree + 3.0) / (degree + 2.0)) * (u * nxt)
                    - ((degree + 1.0) / (degree + 2.0)) * now
                )
            oper[side, 0, at] = real * scale
            oper[side, 1, at] = imag * scale
            return carry

        lax.fori_loop(0, blocks + (lt // 8 if crossed else 0), oper_step, 0)

    for copy in copies[7:]:
        copy.wait()

    ph2[1] = ph2[1] * (2 * x - 1).astype(jnp.float32)
    if crossed:
        x_copy(0).wait_recv()
        z_start(0, 1)

        @pl.when(turned_order == 0)
        def _():
            y_first().wait_recv()
            z_start(plain, 2)

        @pl.when(turned_order == 1)
        def _():
            for i in range(1, plain):
                z_start(i, 0)
    else:
        for i in range(plain):
            x_copy(i).wait_recv()
            z_start(i, 1)

    lanes = lax.broadcasted_iota(jnp.int32, (slab, lp), 1)
    odd_lane = lanes % 2 == 1
    late_lane = lanes % 4 >= 2

    def woven(planes):
        pairs = [jnp.where(odd_lane, planes[(k + 1) % 4], planes[k]) for k in range(4)]
        mixed = [jnp.where(late_lane, pairs[(2 - h) % 4], pairs[-h % 4]) for h in range(4)]
        return [mixed[h] if h == 0 else pltpu.roll(mixed[h], lp - h, 1) for h in range(4)]

    def first_level(unit, place):
        source = jnp.concatenate(
            [taken[side, unit, place].reshape(4 * lt, lp) for side in range(2)], axis=0
        )
        high, low = split(source)
        both = dot(jnp.concatenate([high, low], axis=1), c1[...])
        odd_high, odd_low = split(both[:, :lp] + both[:, lp:])
        high = jnp.concatenate([high, odd_high], axis=1)
        low = jnp.concatenate([low, odd_low], axis=1)
        done = []
        cosine, sine = ph1[0], ph1[1]
        for side in range(2):
            parts = []
            for k in range(4):
                at = slice((4 * side + k) * lt, (4 * side + k + 1) * lt)
                parts.append(
                    dot(r1[...], jnp.concatenate([high[at], low[at], high[at]], axis=0))
                )
            sr, si, dre, dim = parts
            done.append((cosine * sr - sine * dim, cosine * si + sine * dre))
        return done

    def keep_own(unit):
        for side, (real, imag) in enumerate(first_level(unit, x)):
            first[side, 0] = real
            first[side, 1] = imag

    def unit_at(step):
        if not crossed:
            return 0, step
        kind = 1 - (step + turned_order * (step // 2)) % 2
        return kind, kind * (plain + (dh + step // 2) % 2) + (1 - kind) * (step // 2)

    def slab_at(kind, s):
        if not crossed:
            return box, s, x * rows + s * slab
        top = s // half_n
        low = s % half_n
        to_box = kind * (pair * 2 + top) + (1 - kind) * box
        to_dir = kind * (dh * half_n + low) + (1 - kind) * s
        row = kind * (top * rows + dh * lt + low * slab) + (1 - kind) * (x * rows + s * slab)
        return to_box, to_dir, row

    def slab_number(kind, o):
        if n_dir % 2:
            return (me + 1 + o) % n_dir
        top = kind * x + (1 - kind) * dh
        return (top + 1 - o // half_n) % 2 * half_n + (dl + 1 + o) % half_n

    def whose(kind, unit):
        if not crossed:
            return me * count + unit
        source = (unit - plain) * half_n + dl
        return kind * (source * count + plain + x) + (1 - kind) * (me * count + unit)

    def d_copy(kind, unit, o):
        s = slab_number(kind, o)
        to_box, to_dir, _ = slab_at(kind, s)
        rhs = whose(kind, unit)
        return pltpu.make_async_remote_copy(
            ready.at[unit, s], out.at[rhs], ds.at[unit, o], dr.at[rhs],
            (to_box, to_dir), device_id_type=MESH,
        )

    def do_unit(kind, unit):
        for side, (br, bi) in enumerate(first_level(unit, 1 - x)):
            ar, ai = first[side, 0], first[side, 1]
            for k, value in enumerate((ar + br, ai + bi, ar - br, ai - bi)):
                high, low = split(value)
                wide = dot(r2[kind], jnp.concatenate([high, low, high], axis=0))
                even[side, k] = wide
                high, low = split(wide)
                lhs2[side, k, :, : 2 * lp] = high
                lhs2[side, k, :, 2 * lp :] = low
        for o in range(n_dir):
            s = slab_number(kind, o)
            at = pl.ds(pl.multiple_of(s * slab, slab), slab)
            both = jnp.concatenate(
                [lhs2[side, k, at, :] for side in range(2) for k in range(4)], axis=0
            )
            odd = dot(jnp.concatenate([both, both[:, : 2 * lp]], axis=1), c2[...])
            row = pl.ds(pl.multiple_of(slab_at(kind, s)[2], slab), slab)
            planes = []
            for v in range(4):
                cut = slice(v * lp, (v + 1) * lp)
                cosine, sine = ph2[0, row, cut], ph2[1, row, cut]
                total = None
                for side in range(2):
                    if v < 2:
                        sr, si, dre, dim = [even[side, k, at, cut] for k in range(4)]
                    else:
                        sr, si, dre, dim = [
                            odd[(4 * side + k) * slab : (4 * side + k + 1) * slab,
                                (v - 2) * lp : (v - 1) * lp]
                            for k in range(4)
                        ]
                    gr = cosine * sr - sine * dim
                    gi = cosine * si + sine * dre
                    pr, pi = oper[side, 0, row, cut], oper[side, 1, row, cut]
                    real, imag = pr * gr - pi * gi, pr * gi + pi * gr
                    total = (real, imag) if total is None else (total[0] + real, total[1] + imag)
                planes.append(total)
            for c in range(2):
                parts = woven([planes[v][c] for v in (0, 2, 1, 3)])
                for h in range(4):
                    ready[unit, s, c, :, h * lp : (h + 1) * lp] = parts[h]
            if o == half_n - 1:
                for sent in range(half_n):
                    d_copy(kind, unit, sent).start()
            if o == n_dir - 1:
                for sent in range(half_n, n_dir - 1):
                    d_copy(kind, unit, sent).start()
                out[whose(kind, unit)] = ready[unit, s]

    def level_step(step, carry):
        kind, unit = unit_at(step)
        if crossed:
            @pl.when(step == 0)
            def _():
                y_start()

            @pl.when(step == 2 - turned_order)
            def _():
                for i in range(1, plain):
                    x_copy(i).wait_recv()
                    z_start(i, 1)

        for side, present in ((0, has_lower), (1, has_upper)):
            @pl.when(jnp.logical_and(present, step >= crossed))
            def _():
                arrived(side, unit, 1 - x)

        do_unit(kind, unit)

        @pl.when(step < count - 1)
        def _():
            _, following = unit_at(step + 1)
            for side, present in ((0, has_lower), (1, has_upper)):
                @pl.when(present)
                def _():
                    arrived(side, following, x)

            keep_own(following)

        return carry

    _, beginning = unit_at(0)
    for side, present in ((0, has_lower), (1, has_upper)):
        @pl.when(present)
        def _():
            arrived(side, beginning, x)
            if crossed:
                @pl.when(turned_order == 1)
                def _():
                    y_copy(side, x, 1).start()

    keep_own(beginning)
    lax.fori_loop(0, count, level_step, 0)

    def out_arrived(rhs):
        pltpu.make_async_remote_copy(
            ready.at[0, 0], out.at[rhs], ds.at[0, 0], dr.at[rhs],
            (box, across), device_id_type=MESH,
        ).wait_recv()

    for step in range(count):
        kind, unit = unit_at(step)
        for o in range(n_dir - 1):
            d_copy(kind, unit, o).wait_send()
    for o in range(1, n_dir):
        for r in range(plain):
            out_arrived((me + o) % n_dir * count + r)
        if crossed:
            s = (x * half_n + dl + o) % n_dir
            for k in range(2):
                out_arrived((k * half_n + s % half_n) * count + plain + s // half_n)
    for i in range(plain):
        x_copy(i).wait_send()
    if crossed:
        @pl.when(turned_order == 0)
        def _():
            y_first().wait_send()

    for side, sends, gets in ((0, has_upper, has_lower), (1, has_lower, has_upper)):
        @pl.when(sends)
        def _():
            for i in range(plain + crossed):
                for passed in range(2):
                    z_copy(i, passed, side).wait_send()
            if crossed:
                @pl.when(turned_order == 0)
                def _():
                    z_copy(plain, 2, side).wait_send()

        if crossed:
            @pl.when(gets)
            def _():
                y_copy(side, 1 - x, 0).wait_send()

                @pl.when(turned_order == 1)
                def _():
                    y_copy(side, x, 1).wait_send()


def per_device(n_box, n_dir, leaf_patterns, occupancy, pair_lists):
    _, count, _, lt, lp = leaf_patterns.shape
    assert leaf_patterns.shape[0] == 2
    slab = 2 * lt // n_dir
    crossed = int(count == 4 and n_dir % 2 == 0)
    steps = count - crossed
    bf16 = jnp.bfloat16
    lane = np.arange(lp)
    order = []
    for s in range(4):
        h = (lane % 4 - s) % 4
        order.append(lp * h + (lane - h) % lp)
    turn = (order[0] // 4).astype(np.int32)[None]
    first_order = np.concatenate([order[0], order[2]]) // 2
    second_odd = np.concatenate([order[1], order[3]])
    second_order = np.concatenate([order[0], order[2], second_odd])
    high, low = halves(interp_table(lp, 0.0)[first_order[lp:]][:, turn[0]].T)
    c1 = np.concatenate([np.concatenate([high, low], axis=1)] * 2, axis=0)
    row_high, row_low = halves(interp_table(lt, 0.5))
    r1 = np.concatenate([row_high, row_high, row_low], axis=1)
    row_high, row_low = halves(interp_table(2 * lt, 0.5))
    r2 = np.concatenate([row_high, row_high, row_low], axis=1)
    high, low = halves(interp_table(2 * lp, 0.0)[second_odd][:, first_order].T)
    c2 = np.concatenate([high, high, low], axis=0)
    st, _, cp, _ = sines(2 * lt, 2 * lp)
    angle = phase_first * st[:, None] * cp[first_order][None]
    ph1 = np.stack([np.cos(angle), np.sin(angle)]).astype(np.float32)
    st, ct, cp, sp = sines(4 * lt, 4 * lp)
    cp, sp = cp[second_order], sp[second_order]
    angle = phase_second * st[:, None] * sp[None]
    ph2 = np.stack([np.cos(angle), np.sin(angle)]).astype(np.float32)
    polar = np.stack([st, ct])[:, :, None].astype(np.float32)
    azim = np.stack([cp, sp]).astype(np.float32)
    series = series_table(n_box // 2)
    operands = (
        leaf_patterns, occupancy, pair_lists, series, c1, r1, r2, c2, ph1, ph2, polar, azim,
        turn,
    )
    chunk = (2, slab, 4 * lp)
    f32 = jnp.float32
    rows = 2 * lt
    result = pl.pallas_call(
        functools.partial(kernel, (n_box, n_dir, count, lt, lp, slab, crossed)),
        out_shape=jax.ShapeDtypeStruct((n_dir * count,) + chunk, f32),
        in_specs=[pl.BlockSpec(memory_space=pltpu.HBM)] * len(operands),
        out_specs=pl.BlockSpec(memory_space=pltpu.VMEM),
        scratch_shapes=[
            pltpu.VMEM(leaf_patterns.shape, f32),
            pltpu.SMEM(occupancy.shape, jnp.int32),
            pltpu.SMEM(pair_lists.shape, jnp.int32),
            pltpu.SMEM(series.shape, f32),
            pltpu.VMEM(c1.shape, bf16),
            pltpu.VMEM(r1.shape, bf16),
            pltpu.VMEM((1 + crossed, rows) + r2.shape[1:], bf16),
            pltpu.VMEM(c2.shape, bf16),
            pltpu.VMEM(ph1.shape, f32),
            pltpu.VMEM(ph2.shape, f32),
            pltpu.VMEM(polar.shape, f32),
            pltpu.VMEM(azim.shape, f32),
            pltpu.VMEM(turn.shape, jnp.int32),
            pltpu.VMEM((count, 4, lt, lp), f32),
            pltpu.VMEM((steps, 4, lt, lp), f32),
            pltpu.VMEM((4, lt, lp), f32),
            pltpu.VMEM((2, count, 2, 4, lt, lp), f32),
            pltpu.VMEM((2, 2, rows, 2 * lp), f32),
            pltpu.VMEM((2, 4, rows, 4 * lp), bf16),
            pltpu.VMEM((2, 4, rows, 2 * lp), f32),
            pltpu.VMEM((count, n_dir) + chunk, f32),
            pltpu.VMEM((2, 2, 2 * rows, 4 * lp), f32),
            pltpu.SemaphoreType.DMA((len(operands) + 2 * crossed,)),
            pltpu.SemaphoreType.DMA((steps,)),
            pltpu.SemaphoreType.DMA((steps,)),
            pltpu.SemaphoreType.DMA((2, count, 3)),
            pltpu.SemaphoreType.DMA((2, count, 2)),
            pltpu.SemaphoreType.DMA((6,)),
            pltpu.SemaphoreType.DMA((count, n_dir)),
            pltpu.SemaphoreType.DMA((n_dir * count,)),
        ],
        compiler_params=pltpu.CompilerParams(
            collective_id=0, has_side_effects=True, vmem_limit_bytes=48 << 20
        ),
    )(*[pltpu.with_memory_space_constraint(jnp.asarray(operand), pltpu.HBM) for operand in operands])
    return result.reshape(1, 1, n_dir * count, *chunk)


def solution(mesh):
    placed = (P("box", "dir", None, None, None), P("box"), P())
    return jax.shard_map(
        functools.partial(per_device, mesh.shape["box"], mesh.shape["dir"]),
        mesh=mesh,
        in_specs=placed,
        out_specs=P("box", None, None, None, "dir", None),
        check_vma=False,
    )
```

```python
import functools

import jax
import jax.numpy as jnp
import numpy as np
from jax import lax
from jax.experimental import pallas as pl
from jax.experimental.pallas import tpu as pltpu
from jax.sharding import PartitionSpec as P

MESH = pl.DeviceIdType.MESH
LTR = 16
full_count = 16.0
phase_first = 16.0
phase_second = 64.0
translate_wave = 20.0


def interp_table(points, offset):
    orders = np.arange(points // 2 + 1, dtype=np.float64)
    weights = np.where((orders == 0) | (orders == points // 2), 1.0, 2.0) / points
    source = (np.arange(points) + offset) / points
    target = (np.arange(2 * points) + offset) / (2 * points)
    angle = 2.0 * np.pi * (target[:, None, None] - source[None, :, None]) * orders
    return (np.cos(angle) * weights).sum(-1)


def halves(table):
    high = np.asarray(table, np.float32).astype(jnp.bfloat16)
    low = (np.asarray(table, np.float64) - high.astype(np.float64)).astype(jnp.bfloat16)
    return high, low


def sines(rows, columns):
    theta = np.pi * (np.arange(rows) + 0.5) / rows
    phi = 2.0 * np.pi * np.arange(columns) / columns
    return np.sin(theta), np.cos(theta), np.cos(phi), np.sin(phi)


def center(g):
    return np.array([g % 4, g // 4 % 4, g // 16], np.float64)


def series_table(pairs):
    table = np.zeros((pairs, 2 * (3 + 2 * (LTR + 1))), np.float64)
    width = 3 + 2 * (LTR + 1)
    for g in range(pairs):
        for side, s in enumerate((g - 1, g + 1)):
            if not 0 <= s < pairs:
                continue
            r = center(g) - center(s)
            distance = np.sqrt((r * r).sum())
            x = translate_wave * distance
            now = (np.sin(x) - 1j * np.cos(x)) / x
            nxt = ((np.sin(x) - x * np.cos(x)) - 1j * (x * np.sin(x) + np.cos(x))) / x**2
            table[g, side * width : side * width + 3] = r / distance
            for degree in range(LTR + 1):
                value = (1j**degree) * (2 * degree + 1) * now
                table[g, side * width + 3 + 2 * degree] = value.real
                table[g, side * width + 4 + 2 * degree] = value.imag
                now, nxt = nxt, (2 * degree + 3) / x * nxt - now
    return table.astype(np.float32)


def split(value):
    high = value.astype(jnp.bfloat16)
    low = (value - high.astype(jnp.float32)).astype(jnp.bfloat16)
    return high, low


def dot(a, b):
    return jnp.dot(a, b, preferred_element_type=jnp.float32)


def kernel(
    sizes,
    leaf_in, occ_in, lists_in, series_in, c1_in, r1_in, r2_in, c2_in, ph1_in, ph2_in,
    polar_in, azim_in, turn_in,
    out,
    leaf, occ, lists, series, c1, r1, r2, c2, ph1, ph2, polar, azim, turn,
    mine, gath, yours, taken, first, lhs2, even, ready, oper,
    loads, xs, xr, ls, lr, ys, ds, dr,
):
    n_box, n_dir, count, lt, lp, slab, crossed = sizes
    plain = count - 2 * crossed
    half_n = n_dir // 2
    rows = 2 * lt
    box = lax.axis_index("box")
    me = lax.axis_index("dir")
    x = box % 2
    pair = box // 2
    dh = me // half_n
    dl = me % half_n
    turned_order = (dl + 1) % 2
    has_lower = pair > 0
    has_upper = pair < n_box // 2 - 1
    partner = box + 1 - 2 * x
    across = (me + half_n) % n_dir

    start_own = pl.multiple_of(x * rows, rows)
    pairs_in = [
        (leaf_in, leaf), (occ_in, occ), (turn_in, turn), (lists_in, lists), (series_in, series),
        (polar_in, polar), (azim_in, azim), (c1_in, c1), (r1_in, r1),
        (ph1_in, ph1), (c2_in, c2), (ph2_in, ph2),
        (r2_in.at[pl.ds(start_own, rows)], r2.at[0]),
    ]
    if crossed:
        for k in range(2):
            start = pl.multiple_of(k * rows + dh * lt, lt)
            pairs_in.append((r2_in.at[pl.ds(start, lt)], r2.at[1, pl.ds(k * lt, lt)]))
    copies = [
        pltpu.make_async_copy(source, target, loads.at[i])
        for i, (source, target) in enumerate(pairs_in)
    ]
    for copy in copies[:3]:
        copy.start()
    barrier = pltpu.get_barrier_semaphore()
    for o in range(1, n_dir):
        pl.semaphore_signal(
            barrier, inc=1, device_id=(box, (me + o) % n_dir), device_id_type=MESH
        )
    if crossed:
        for k in range(half_n):
            pl.semaphore_signal(
                barrier, inc=1, device_id=(partner, dh * half_n + k), device_id_type=MESH
            )
        for present, by in ((has_lower, -2), (has_upper, 2)):
            @pl.when(present)
            def _():
                pl.semaphore_signal(
                    barrier, inc=1, device_id=(partner + by, me), device_id_type=MESH
                )
    else:
        pl.semaphore_signal(barrier, inc=1, device_id=(partner, me), device_id_type=MESH)
    for present, by in ((has_lower, -2), (has_upper, 2)):
        @pl.when(present)
        def _():
            pl.semaphore_signal(barrier, inc=1, device_id=(box + by, me), device_id_type=MESH)

    for copy in copies[3:]:
        copy.start()
    for copy in copies[:3]:
        copy.wait()

    w0 = occ[0].astype(jnp.float32) / full_count
    w1 = occ[1].astype(jnp.float32) / full_count
    turned = jnp.broadcast_to(turn[...], (lt, lp))
    for r in range(count):
        for c in range(2):
            a = jnp.take_along_axis(leaf[0, r, c], turned, axis=1) * w0
            b = jnp.take_along_axis(leaf[1, r, c], turned, axis=1) * w1
            mine[r, c] = a + b
            mine[r, 2 + c] = b - a

    pl.semaphore_wait(
        barrier,
        n_dir - 1 + (half_n if crossed else 1)
        + (1 + crossed) * (has_lower.astype(jnp.int32) + has_upper.astype(jnp.int32)),
    )

    def x_copy(i):
        return pltpu.make_async_remote_copy(
            mine.at[i], gath.at[i], xs.at[i], xr.at[i], (partner, me), device_id_type=MESH
        )

    def z_copy(i, passed, side):
        by = 2 - 4 * side
        target = box + by
        if i == plain:
            unit = plain + dh
            source, place = mine.at[plain + x], x
            if passed == 1:
                source, target = mine.at[plain + 1 - x], partner + by
            elif passed == 2:
                source, unit = yours, plain + 1 - dh
        else:
            unit = i
            source, place = (gath.at[i], 1 - x) if passed else (mine.at[i], x)
        return pltpu.make_async_remote_copy(
            source, taken.at[side, unit, place], ls.at[side, i, passed],
            lr.at[side, unit, place], (target, me), device_id_type=MESH,
        )

    def z_start(i, passed):
        @pl.when(has_upper)
        def _():
            z_copy(i, passed, 0).start()

        @pl.when(has_lower)
        def _():
            z_copy(i, passed, 1).start()

    def arrived(side, unit, place):
        pltpu.make_async_remote_copy(
            mine.at[0], taken.at[side, unit, place], ls.at[side, 0, 0],
            lr.at[side, unit, place], (partner, me), device_id_type=MESH,
        ).wait_recv()

    def y_first():
        return pltpu.make_async_remote_copy(
            mine.at[plain + x], yours, ys.at[4], ys.at[5], (box, across),
            device_id_type=MESH,
        )

    def y_copy(side, place, sent):
        block = taken.at[side, plain + dh, place]
        return pltpu.make_async_remote_copy(
            block, block, ys.at[2 * sent + side], lr.at[side, plain + dh, place],
            (box, across), device_id_type=MESH,
        )

    def y_start():
        for side, present in ((0, has_lower), (1, has_upper)):
            @pl.when(present)
            def _():
                arrived(side, plain + dh, 1 - x)
                y_copy(side, 1 - x, 0).start()

    if crossed:
        @pl.when(turned_order == 0)
        def _():
            y_first().start()

        z_start(plain, 0)
        z_start(plain, 1)
        x_copy(0).start()
        z_start(0, 0)
        for i in range(1, plain):
            x_copy(i).start()

        @pl.when(turned_order == 0)
        def _():
            for i in range(1, plain):
                z_start(i, 0)

    else:
        for i in range(plain):
            x_copy(i).start()
            z_start(i, 0)

    for side, present in ((0, has_lower), (1, has_upper)):
        @pl.when(jnp.logical_not(present))
        def _():
            taken[side] = jnp.zeros(taken.shape[1:], jnp.float32)

    for copy in copies[3:7]:
        copy.wait()

    slots = lists.shape[1]
    entries = lists.shape[2]
    width = 3 + 2 * (LTR + 1)
    blocks = rows // 8
    for side, present in ((0, has_lower), (1, has_upper)):
        named = jnp.float32(0.0)
        for k in range(entries):
            chosen = lists[pair, 0, k]
            hit = chosen < slots if side == 0 else chosen >= 2 * slots
            named = named + jnp.where(hit, 1.0, 0.0)
        scale = named / entries
        base = side * width

        def oper_step(i, carry):
            other = i // blocks
            start = (x + other) % 2 * rows + other * dh * lt + i % blocks * 8
            at = pl.ds(pl.multiple_of(start, 8), 8)
            along_x = polar[0, at] * azim[0:1]
            along_y = polar[0, at] * azim[1:2]
            along_z = polar[1, at] * jnp.ones_like(along_x)
            u = (
                series[pair, base] * along_x
                + series[pair, base + 1] * along_y
                + series[pair, base + 2] * along_z
            )
            now, nxt = jnp.ones_like(u), u
            real, imag = jnp.zeros_like(u), jnp.zeros_like(u)
            for degree in range(LTR + 1):
                real = real + series[pair, base + 3 + 2 * degree] * now
                imag = imag + series[pair, base + 4 + 2 * degree] * now
                now, nxt = nxt, (
                    ((2.0 * degree + 3.0) / (degree + 2.0)) * (u * nxt)
                    - ((degree + 1.0) / (degree + 2.0)) * now
                )
            oper[side, 0, at] = real * scale
            oper[side, 1, at] = imag * scale
            return carry

        lax.fori_loop(0, blocks + (lt // 8 if crossed else 0), oper_step, 0)

    for copy in copies[7:]:
        copy.wait()

    ph2[1] = ph2[1] * (2 * x - 1).astype(jnp.float32)
    if crossed:
        x_copy(0).wait_recv()
        z_start(0, 1)

        @pl.when(turned_order == 0)
        def _():
            y_first().wait_recv()
            z_start(plain, 2)

        @pl.when(turned_order == 1)
        def _():
            for i in range(1, plain):
                z_start(i, 0)
    else:
        for i in range(plain):
            x_copy(i).wait_recv()
            z_start(i, 1)

    lanes = lax.broadcasted_iota(jnp.int32, (slab, lp), 1)
    odd_lane = lanes % 2 == 1
    late_lane = lanes % 4 >= 2

    def woven(planes):
        pairs = [jnp.where(odd_lane, planes[(k + 1) % 4], planes[k]) for k in range(4)]
        mixed = [jnp.where(late_lane, pairs[(2 - h) % 4], pairs[-h % 4]) for h in range(4)]
        return [mixed[h] if h == 0 else pltpu.roll(mixed[h], lp - h, 1) for h in range(4)]

    def first_level(unit, place):
        source = jnp.concatenate(
            [taken[side, unit, place].reshape(4 * lt, lp) for side in range(2)], axis=0
        )
        high, low = split(source)
        both = dot(jnp.concatenate([high, low], axis=1), c1[...])
        odd_high, odd_low = split(both[:, :lp] + both[:, lp:])
        high = jnp.concatenate([high, odd_high], axis=1)
        low = jnp.concatenate([low, odd_low], axis=1)
        done = []
        cosine, sine = ph1[0], ph1[1]
        for side in range(2):
            parts = []
            for k in range(4):
                at = slice((4 * side + k) * lt, (4 * side + k + 1) * lt)
                parts.append(
                    dot(r1[...], jnp.concatenate([high[at], low[at], high[at]], axis=0))
                )
            sr, si, dre, dim = parts
            done.append((cosine * sr - sine * dim, cosine * si + sine * dre))
        return done

    def keep_own(unit):
        for side, (real, imag) in enumerate(first_level(unit, x)):
            first[side, 0] = real
            first[side, 1] = imag

    def unit_at(step):
        if not crossed:
            return 0, step
        kind = 1 - (step + turned_order * (step // 2)) % 2
        return kind, kind * (plain + (dh + step // 2) % 2) + (1 - kind) * (step // 2)

    def slab_at(kind, s):
        if not crossed:
            return box, s, x * rows + s * slab
        top = s // half_n
        low = s % half_n
        to_box = kind * (pair * 2 + top) + (1 - kind) * box
        to_dir = kind * (dh * half_n + low) + (1 - kind) * s
        row = kind * (top * rows + dh * lt + low * slab) + (1 - kind) * (x * rows + s * slab)
        return to_box, to_dir, row

    def slab_number(kind, o):
        if n_dir % 2:
            return (me + 1 + o) % n_dir
        top = kind * x + (1 - kind) * dh
        return (top + 1 - o // half_n) % 2 * half_n + (dl + 1 + o) % half_n

    def whose(kind, unit):
        if not crossed:
            return me * count + unit
        source = (unit - plain) * half_n + dl
        return kind * (source * count + plain + x) + (1 - kind) * (me * count + unit)

    def d_copy(kind, unit, o):
        s = slab_number(kind, o)
        to_box, to_dir, _ = slab_at(kind, s)
        rhs = whose(kind, unit)
        return pltpu.make_async_remote_copy(
            ready.at[unit, s], out.at[rhs], ds.at[unit, o], dr.at[rhs],
            (to_box, to_dir), device_id_type=MESH,
        )

    def do_unit(kind, unit):
        for side, (br, bi) in enumerate(first_level(unit, 1 - x)):
            ar, ai = first[side, 0], first[side, 1]
            for k, value in enumerate((ar + br, ai + bi, ar - br, ai - bi)):
                high, low = split(value)
                wide = dot(r2[kind], jnp.concatenate([high, low, high], axis=0))
                even[side, k] = wide
                high, low = split(wide)
                lhs2[side, k, :, : 2 * lp] = high
                lhs2[side, k, :, 2 * lp :] = low
        for o in range(n_dir):
            s = slab_number(kind, o)
            at = pl.ds(pl.multiple_of(s * slab, slab), slab)
            both = jnp.concatenate(
                [lhs2[side, k, at, :] for side in range(2) for k in range(4)], axis=0
            )
            odd = dot(jnp.concatenate([both, both[:, : 2 * lp]], axis=1), c2[...])
            row = pl.ds(pl.multiple_of(slab_at(kind, s)[2], slab), slab)
            planes = []
            for v in range(4):
                cut = slice(v * lp, (v + 1) * lp)
                cosine, sine = ph2[0, row, cut], ph2[1, row, cut]
                total = None
                for side in range(2):
                    if v < 2:
                        sr, si, dre, dim = [even[side, k, at, cut] for k in range(4)]
                    else:
                        sr, si, dre, dim = [
                            odd[(4 * side + k) * slab : (4 * side + k + 1) * slab,
                                (v - 2) * lp : (v - 1) * lp]
                            for k in range(4)
                        ]
                    gr = cosine * sr - sine * dim
                    gi = cosine * si + sine * dre
                    pr, pi = oper[side, 0, row, cut], oper[side, 1, row, cut]
                    real, imag = pr * gr - pi * gi, pr * gi + pi * gr
                    total = (real, imag) if total is None else (total[0] + real, total[1] + imag)
                planes.append(total)
            for c in range(2):
                parts = woven([planes[v][c] for v in (0, 2, 1, 3)])
                for h in range(4):
                    ready[unit, s, c, :, h * lp : (h + 1) * lp] = parts[h]
            if o == half_n - 1:
                for sent in range(half_n):
                    d_copy(kind, unit, sent).start()
            if o == n_dir - 1:
                for sent in range(half_n, n_dir - 1):
                    d_copy(kind, unit, sent).start()
                out[whose(kind, unit)] = ready[unit, s]

    def level_step(step, carry):
        kind, unit = unit_at(step)
        if crossed:
            @pl.when(step == 0)
            def _():
                y_start()

            @pl.when(step == 2 - turned_order)
            def _():
                for i in range(1, plain):
                    x_copy(i).wait_recv()
                    z_start(i, 1)

        for side, present in ((0, has_lower), (1, has_upper)):
            @pl.when(jnp.logical_and(present, step >= crossed))
            def _():
                arrived(side, unit, 1 - x)

        do_unit(kind, unit)

        @pl.when(step < count - 1)
        def _():
            _, following = unit_at(step + 1)
            for side, present in ((0, has_lower), (1, has_upper)):
                @pl.when(present)
                def _():
                    arrived(side, following, x)

            keep_own(following)

        return carry

    _, beginning = unit_at(0)
    for side, present in ((0, has_lower), (1, has_upper)):
        @pl.when(present)
        def _():
            arrived(side, beginning, x)
            if crossed:
                @pl.when(turned_order == 1)
                def _():
                    y_copy(side, x, 1).start()

    keep_own(beginning)
    lax.fori_loop(0, count, level_step, 0)

    def out_arrived(rhs):
        pltpu.make_async_remote_copy(
            ready.at[0, 0], out.at[rhs], ds.at[0, 0], dr.at[rhs],
            (box, across), device_id_type=MESH,
        ).wait_recv()

    for step in range(count):
        kind, unit = unit_at(step)
        for o in range(n_dir - 1):
            d_copy(kind, unit, o).wait_send()
    for o in range(1, n_dir):
        for r in range(plain):
            out_arrived((me + o) % n_dir * count + r)
        if crossed:
            s = (x * half_n + dl + o) % n_dir
            for k in range(2):
                out_arrived((k * half_n + s % half_n) * count + plain + s // half_n)
    for i in range(plain):
        x_copy(i).wait_send()
    if crossed:
        @pl.when(turned_order == 0)
        def _():
            y_first().wait_send()

    for side, sends, gets in ((0, has_upper, has_lower), (1, has_lower, has_upper)):
        @pl.when(sends)
        def _():
            for i in range(plain + crossed):
                for passed in range(2):
                    z_copy(i, passed, side).wait_send()
            if crossed:
                @pl.when(turned_order == 0)
                def _():
                    z_copy(plain, 2, side).wait_send()

        if crossed:
            @pl.when(gets)
            def _():
                y_copy(side, 1 - x, 0).wait_send()

                @pl.when(turned_order == 1)
                def _():
                    y_copy(side, x, 1).wait_send()


def per_device(n_box, n_dir, leaf_patterns, occupancy, pair_lists):
    _, count, _, lt, lp = leaf_patterns.shape
    assert leaf_patterns.shape[0] == 2
    slab = 2 * lt // n_dir
    crossed = int(count == 4 and n_dir % 2 == 0)
    steps = count - crossed
    bf16 = jnp.bfloat16
    lane = np.arange(lp)
    order = []
    for s in range(4):
        h = (lane % 4 - s) % 4
        order.append(lp * h + (lane - h) % lp)
    turn = (order[0] // 4).astype(np.int32)[None]
    first_order = np.concatenate([order[0], order[2]]) // 2
    second_odd = np.concatenate([order[1], order[3]])
    second_order = np.concatenate([order[0], order[2], second_odd])
    high, low = halves(interp_table(lp, 0.0)[first_order[lp:]][:, turn[0]].T)
    c1 = np.concatenate([np.concatenate([high, low], axis=1)] * 2, axis=0)
    row_high, row_low = halves(interp_table(lt, 0.5))
    r1 = np.concatenate([row_high, row_high, row_low], axis=1)
    row_high, row_low = halves(interp_table(2 * lt, 0.5))
    r2 = np.concatenate([row_high, row_high, row_low], axis=1)
    high, low = halves(interp_table(2 * lp, 0.0)[second_odd][:, first_order].T)
    c2 = np.concatenate([high, high, low], axis=0)
    st, _, cp, _ = sines(2 * lt, 2 * lp)
    angle = phase_first * st[:, None] * cp[first_order][None]
    ph1 = np.stack([np.cos(angle), np.sin(angle)]).astype(np.float32)
    st, ct, cp, sp = sines(4 * lt, 4 * lp)
    cp, sp = cp[second_order], sp[second_order]
    angle = phase_second * st[:, None] * sp[None]
    ph2 = np.stack([np.cos(angle), np.sin(angle)]).astype(np.float32)
    polar = np.stack([st, ct])[:, :, None].astype(np.float32)
    azim = np.stack([cp, sp]).astype(np.float32)
    series = series_table(n_box // 2)
    operands = (
        leaf_patterns, occupancy, pair_lists, series, c1, r1, r2, c2, ph1, ph2, polar, azim,
        turn,
    )
    chunk = (2, slab, 4 * lp)
    f32 = jnp.float32
    rows = 2 * lt
    result = pl.pallas_call(
        functools.partial(kernel, (n_box, n_dir, count, lt, lp, slab, crossed)),
        out_shape=jax.ShapeDtypeStruct((n_dir * count,) + chunk, f32),
        in_specs=[pl.BlockSpec(memory_space=pltpu.HBM)] * len(operands),
        out_specs=pl.BlockSpec(memory_space=pltpu.VMEM),
        scratch_shapes=[
            pltpu.VMEM(leaf_patterns.shape, f32),
            pltpu.SMEM(occupancy.shape, jnp.int32),
            pltpu.SMEM(pair_lists.shape, jnp.int32),
            pltpu.SMEM(series.shape, f32),
            pltpu.VMEM(c1.shape, bf16),
            pltpu.VMEM(r1.shape, bf16),
            pltpu.VMEM((1 + crossed, rows) + r2.shape[1:], bf16),
            pltpu.VMEM(c2.shape, bf16),
            pltpu.VMEM(ph1.shape, f32),
            pltpu.VMEM(ph2.shape, f32),
            pltpu.VMEM(polar.shape, f32),
            pltpu.VMEM(azim.shape, f32),
            pltpu.VMEM(turn.shape, jnp.int32),
            pltpu.VMEM((count, 4, lt, lp), f32),
            pltpu.VMEM((steps, 4, lt, lp), f32),
            pltpu.VMEM((4, lt, lp), f32),
            pltpu.VMEM((2, count, 2, 4, lt, lp), f32),
            pltpu.VMEM((2, 2, rows, 2 * lp), f32),
            pltpu.VMEM((2, 4, rows, 4 * lp), bf16),
            pltpu.VMEM((2, 4, rows, 2 * lp), f32),
            pltpu.VMEM((count, n_dir) + chunk, f32),
            pltpu.VMEM((2, 2, 2 * rows, 4 * lp), f32),
            pltpu.SemaphoreType.DMA((len(operands) + 2 * crossed,)),
            pltpu.SemaphoreType.DMA((steps,)),
            pltpu.SemaphoreType.DMA((steps,)),
            pltpu.SemaphoreType.DMA((2, count, 3)),
            pltpu.SemaphoreType.DMA((2, count, 2)),
            pltpu.SemaphoreType.DMA((6,)),
            pltpu.SemaphoreType.DMA((count, n_dir)),
            pltpu.SemaphoreType.DMA((n_dir * count,)),
        ],
        compiler_params=pltpu.CompilerParams(
            collective_id=0, has_side_effects=True, vmem_limit_bytes=48 << 20
        ),
    )(*[pltpu.with_memory_space_constraint(jnp.asarray(operand), pltpu.HBM) for operand in operands])
    return result.reshape(1, 1, n_dir * count, *chunk)


def solution(mesh):
    placed = (P("box", "dir", None, None, None), P("box"), P())
    return jax.shard_map(
        functools.partial(per_device, mesh.shape["box"], mesh.shape["dir"]),
        mesh=mesh,
        in_specs=placed,
        out_specs=P("box", None, None, None, "dir", None),
        check_vma=False,
    )
```

```python
import functools

import jax
import jax.numpy as jnp
import numpy as np
from jax import lax
from jax.experimental import pallas as pl
from jax.experimental.pallas import tpu as pltpu
from jax.sharding import PartitionSpec as P

MESH = pl.DeviceIdType.MESH
LTR = 16
full_count = 16.0
phase_first = 16.0
phase_second = 64.0
translate_wave = 20.0


def interp_table(points, offset):
    orders = np.arange(points // 2 + 1, dtype=np.float64)
    weights = np.where((orders == 0) | (orders == points // 2), 1.0, 2.0) / points
    source = (np.arange(points) + offset) / points
    target = (np.arange(2 * points) + offset) / (2 * points)
    angle = 2.0 * np.pi * (target[:, None, None] - source[None, :, None]) * orders
    return (np.cos(angle) * weights).sum(-1)


def halves(table):
    high = np.asarray(table, np.float32).astype(jnp.bfloat16)
    low = (np.asarray(table, np.float64) - high.astype(np.float64)).astype(jnp.bfloat16)
    return high, low


def sines(rows, columns):
    theta = np.pi * (np.arange(rows) + 0.5) / rows
    phi = 2.0 * np.pi * np.arange(columns) / columns
    return np.sin(theta), np.cos(theta), np.cos(phi), np.sin(phi)


def center(g):
    return np.array([g % 4, g // 4 % 4, g // 16], np.float64)


def series_table(pairs):
    table = np.zeros((pairs, 2 * (3 + 2 * (LTR + 1))), np.float64)
    width = 3 + 2 * (LTR + 1)
    for g in range(pairs):
        for side, s in enumerate((g - 1, g + 1)):
            if not 0 <= s < pairs:
                continue
            r = center(g) - center(s)
            distance = np.sqrt((r * r).sum())
            x = translate_wave * distance
            now = (np.sin(x) - 1j * np.cos(x)) / x
            nxt = ((np.sin(x) - x * np.cos(x)) - 1j * (x * np.sin(x) + np.cos(x))) / x**2
            table[g, side * width : side * width + 3] = r / distance
            for degree in range(LTR + 1):
                value = (1j**degree) * (2 * degree + 1) * now
                table[g, side * width + 3 + 2 * degree] = value.real
                table[g, side * width + 4 + 2 * degree] = value.imag
                now, nxt = nxt, (2 * degree + 3) / x * nxt - now
    return table.astype(np.float32)


def split(value):
    high = value.astype(jnp.bfloat16)
    low = (value - high.astype(jnp.float32)).astype(jnp.bfloat16)
    return high, low


def dot(a, b):
    return jnp.dot(a, b, preferred_element_type=jnp.float32)


def kernel(
    sizes,
    leaf_in, occ_in, lists_in, series_in, c1_in, r1_in, r2_in, c2_in, ph1_in, ph2_in,
    polar_in, azim_in, turn_in,
    out,
    leaf, occ, lists, series, c1, r1, r2, c2, ph1, ph2, polar, azim, turn,
    mine, gath, yours, taken, first, lhs2, even, ready, oper,
    loads, xs, xr, ls, lr, ys, ds, dr,
):
    n_box, n_dir, count, lt, lp, slab, crossed = sizes
    plain = count - 2 * crossed
    half_n = n_dir // 2
    rows = 2 * lt
    box = lax.axis_index("box")
    me = lax.axis_index("dir")
    x = box % 2
    pair = box // 2
    dh = me // half_n
    dl = me % half_n
    turned_order = (dl + 1) % 2
    has_lower = pair > 0
    has_upper = pair < n_box // 2 - 1
    partner = box + 1 - 2 * x
    across = (me + half_n) % n_dir

    barrier = pltpu.get_barrier_semaphore()
    for o in range(1, n_dir):
        pl.semaphore_signal(
            barrier, inc=1, device_id=(box, (me + o) % n_dir), device_id_type=MESH
        )
    if crossed:
        for k in range(half_n):
            pl.semaphore_signal(
                barrier, inc=1, device_id=(partner, dh * half_n + k), device_id_type=MESH
            )
        for present, by in ((has_lower, -2), (has_upper, 2)):
            @pl.when(present)
            def _():
                pl.semaphore_signal(
                    barrier, inc=1, device_id=(partner + by, me), device_id_type=MESH
                )
    else:
        pl.semaphore_signal(barrier, inc=1, device_id=(partner, me), device_id_type=MESH)
    for present, by in ((has_lower, -2), (has_upper, 2)):
        @pl.when(present)
        def _():
            pl.semaphore_signal(barrier, inc=1, device_id=(box + by, me), device_id_type=MESH)

    start_own = pl.multiple_of(x * rows, rows)
    pairs_in = [
        (leaf_in, leaf), (occ_in, occ), (turn_in, turn), (lists_in, lists), (series_in, series),
        (polar_in, polar), (azim_in, azim), (c1_in, c1), (r1_in, r1),
        (ph1_in, ph1), (c2_in, c2), (ph2_in, ph2),
        (r2_in.at[pl.ds(start_own, rows)], r2.at[0]),
    ]
    if crossed:
        for k in range(2):
            start = pl.multiple_of(k * rows + dh * lt, lt)
            pairs_in.append((r2_in.at[pl.ds(start, lt)], r2.at[1, pl.ds(k * lt, lt)]))
    copies = [
        pltpu.make_async_copy(source, target, loads.at[i])
        for i, (source, target) in enumerate(pairs_in)
    ]
    for copy in copies:
        copy.start()
    for copy in copies[:3]:
        copy.wait()

    w0 = occ[0].astype(jnp.float32) / full_count
    w1 = occ[1].astype(jnp.float32) / full_count
    turned = jnp.broadcast_to(turn[...], (lt, lp))
    for r in range(count):
        for c in range(2):
            a = jnp.take_along_axis(leaf[0, r, c], turned, axis=1) * w0
            b = jnp.take_along_axis(leaf[1, r, c], turned, axis=1) * w1
            mine[r, c] = a + b
            mine[r, 2 + c] = b - a

    pl.semaphore_wait(
        barrier,
        n_dir - 1 + (half_n if crossed else 1)
        + (1 + crossed) * (has_lower.astype(jnp.int32) + has_upper.astype(jnp.int32)),
    )

    def x_copy(i):
        return pltpu.make_async_remote_copy(
            mine.at[i], gath.at[i], xs.at[i], xr.at[i], (partner, me), device_id_type=MESH
        )

    def z_copy(i, passed, side):
        by = 2 - 4 * side
        target = box + by
        if i == plain:
            unit = plain + dh
            source, place = mine.at[plain + x], x
            if passed == 1:
                source, target = mine.at[plain + 1 - x], partner + by
            elif passed == 2:
                source, unit = yours, plain + 1 - dh
        else:
            unit = i
            source, place = (gath.at[i], 1 - x) if passed else (mine.at[i], x)
        return pltpu.make_async_remote_copy(
            source, taken.at[side, unit, place], ls.at[side, i, passed],
            lr.at[side, unit, place], (target, me), device_id_type=MESH,
        )

    def z_start(i, passed):
        @pl.when(has_upper)
        def _():
            z_copy(i, passed, 0).start()

        @pl.when(has_lower)
        def _():
            z_copy(i, passed, 1).start()

    def arrived(side, unit, place):
        pltpu.make_async_remote_copy(
            mine.at[0], taken.at[side, unit, place], ls.at[side, 0, 0],
            lr.at[side, unit, place], (partner, me), device_id_type=MESH,
        ).wait_recv()

    def y_first():
        return pltpu.make_async_remote_copy(
            mine.at[plain + x], yours, ys.at[4], ys.at[5], (box, across),
            device_id_type=MESH,
        )

    def y_copy(side, place, sent):
        block = taken.at[side, plain + dh, place]
        return pltpu.make_async_remote_copy(
            block, block, ys.at[2 * sent + side], lr.at[side, plain + dh, place],
            (box, across), device_id_type=MESH,
        )

    def y_start():
        for side, present in ((0, has_lower), (1, has_upper)):
            @pl.when(present)
            def _():
                arrived(side, plain + dh, 1 - x)
                y_copy(side, 1 - x, 0).start()

    if crossed:
        @pl.when(turned_order == 0)
        def _():
            y_first().start()

        for i in range(plain):
            x_copy(i).start()
        z_start(plain, 0)
        z_start(plain, 1)
        z_start(0, 0)

        @pl.when(turned_order == 0)
        def _():
            for i in range(1, plain):
                z_start(i, 0)

    else:
        for i in range(plain):
            x_copy(i).start()
            z_start(i, 0)

    for side, present in ((0, has_lower), (1, has_upper)):
        @pl.when(jnp.logical_not(present))
        def _():
            taken[side] = jnp.zeros(taken.shape[1:], jnp.float32)

    for copy in copies[3:7]:
        copy.wait()

    slots = lists.shape[1]
    entries = lists.shape[2]
    width = 3 + 2 * (LTR + 1)
    blocks = rows // 8
    for side, present in ((0, has_lower), (1, has_upper)):
        named = jnp.float32(0.0)
        for k in range(entries):
            chosen = lists[pair, 0, k]
            hit = chosen < slots if side == 0 else chosen >= 2 * slots
            named = named + jnp.where(hit, 1.0, 0.0)
        scale = named / entries
        base = side * width

        def oper_step(i, carry):
            other = i // blocks
            start = (x + other) % 2 * rows + other * dh * lt + i % blocks * 8
            at = pl.ds(pl.multiple_of(start, 8), 8)
            along_x = polar[0, at] * azim[0:1]
            along_y = polar[0, at] * azim[1:2]
            along_z = polar[1, at] * jnp.ones_like(along_x)
            u = (
                series[pair, base] * along_x
                + series[pair, base + 1] * along_y
                + series[pair, base + 2] * along_z
            )
            now, nxt = jnp.ones_like(u), u
            real, imag = jnp.zeros_like(u), jnp.zeros_like(u)
            for degree in range(LTR + 1):
                real = real + series[pair, base + 3 + 2 * degree] * now
                imag = imag + series[pair, base + 4 + 2 * degree] * now
                now, nxt = nxt, (
                    ((2.0 * degree + 3.0) / (degree + 2.0)) * (u * nxt)
                    - ((degree + 1.0) / (degree + 2.0)) * now
                )
            oper[side, 0, at] = real * scale
            oper[side, 1, at] = imag * scale
            return carry

        lax.fori_loop(0, blocks + (lt // 8 if crossed else 0), oper_step, 0)

    for copy in copies[7:]:
        copy.wait()

    ph2[1] = ph2[1] * (2 * x - 1).astype(jnp.float32)
    if crossed:
        x_copy(0).wait_recv()
        z_start(0, 1)

        @pl.when(turned_order == 0)
        def _():
            y_first().wait_recv()
            z_start(plain, 2)

        @pl.when(turned_order == 1)
        def _():
            for i in range(1, plain):
                z_start(i, 0)
    else:
        for i in range(plain):
            x_copy(i).wait_recv()
            z_start(i, 1)

    lanes = lax.broadcasted_iota(jnp.int32, (slab, lp), 1)
    odd_lane = lanes % 2 == 1
    late_lane = lanes % 4 >= 2

    def woven(planes):
        pairs = [jnp.where(odd_lane, planes[(k + 1) % 4], planes[k]) for k in range(4)]
        mixed = [jnp.where(late_lane, pairs[(2 - h) % 4], pairs[-h % 4]) for h in range(4)]
        return [mixed[h] if h == 0 else pltpu.roll(mixed[h], lp - h, 1) for h in range(4)]

    def first_level(unit, place):
        source = jnp.concatenate(
            [taken[side, unit, place].reshape(4 * lt, lp) for side in range(2)], axis=0
        )
        high, low = split(source)
        both = dot(jnp.concatenate([high, low], axis=1), c1[...])
        odd_high, odd_low = split(both[:, :lp] + both[:, lp:])
        high = jnp.concatenate([high, odd_high], axis=1)
        low = jnp.concatenate([low, odd_low], axis=1)
        done = []
        cosine, sine = ph1[0], ph1[1]
        for side in range(2):
            parts = []
            for k in range(4):
                at = slice((4 * side + k) * lt, (4 * side + k + 1) * lt)
                parts.append(
                    dot(r1[...], jnp.concatenate([high[at], low[at], high[at]], axis=0))
                )
            sr, si, dre, dim = parts
            done.append((cosine * sr - sine * dim, cosine * si + sine * dre))
        return done

    def keep_own(unit):
        for side, (real, imag) in enumerate(first_level(unit, x)):
            first[side, 0] = real
            first[side, 1] = imag

    def unit_at(step):
        if not crossed:
            return 0, step
        kind = 1 - (step + turned_order * (step // 2)) % 2
        return kind, kind * (plain + (dh + step // 2) % 2) + (1 - kind) * (step // 2)

    def slab_at(kind, s):
        if not crossed:
            return box, s, x * rows + s * slab
        top = s // half_n
        low = s % half_n
        to_box = kind * (pair * 2 + top) + (1 - kind) * box
        to_dir = kind * (dh * half_n + low) + (1 - kind) * s
        row = kind * (top * rows + dh * lt + low * slab) + (1 - kind) * (x * rows + s * slab)
        return to_box, to_dir, row

    def slab_number(kind, o):
        if n_dir % 2:
            return (me + 1 + o) % n_dir
        top = kind * x + (1 - kind) * dh
        return (top + 1 - o // half_n) % 2 * half_n + (dl + 1 + o) % half_n

    def whose(kind, unit):
        if not crossed:
            return me * count + unit
        source = (unit - plain) * half_n + dl
        return kind * (source * count + plain + x) + (1 - kind) * (me * count + unit)

    def d_copy(kind, unit, o):
        s = slab_number(kind, o)
        to_box, to_dir, _ = slab_at(kind, s)
        rhs = whose(kind, unit)
        return pltpu.make_async_remote_copy(
            ready.at[unit, s], out.at[rhs], ds.at[unit, o], dr.at[rhs],
            (to_box, to_dir), device_id_type=MESH,
        )

    def do_unit(kind, unit):
        for side, (br, bi) in enumerate(first_level(unit, 1 - x)):
            ar, ai = first[side, 0], first[side, 1]
            for k, value in enumerate((ar + br, ai + bi, ar - br, ai - bi)):
                high, low = split(value)
                wide = dot(r2[kind], jnp.concatenate([high, low, high], axis=0))
                even[side, k] = wide
                high, low = split(wide)
                lhs2[side, k, :, : 2 * lp] = high
                lhs2[side, k, :, 2 * lp :] = low
        for o in range(n_dir):
            s = slab_number(kind, o)
            at = pl.ds(pl.multiple_of(s * slab, slab), slab)
            both = jnp.concatenate(
                [lhs2[side, k, at, :] for side in range(2) for k in range(4)], axis=0
            )
            odd = dot(jnp.concatenate([both, both[:, : 2 * lp]], axis=1), c2[...])
            row = pl.ds(pl.multiple_of(slab_at(kind, s)[2], slab), slab)
            planes = []
            for v in range(4):
                cut = slice(v * lp, (v + 1) * lp)
                cosine, sine = ph2[0, row, cut], ph2[1, row, cut]
                total = None
                for side in range(2):
                    if v < 2:
                        sr, si, dre, dim = [even[side, k, at, cut] for k in range(4)]
                    else:
                        sr, si, dre, dim = [
                            odd[(4 * side + k) * slab : (4 * side + k + 1) * slab,
                                (v - 2) * lp : (v - 1) * lp]
                            for k in range(4)
                        ]
                    gr = cosine * sr - sine * dim
                    gi = cosine * si + sine * dre
                    pr, pi = oper[side, 0, row, cut], oper[side, 1, row, cut]
                    real, imag = pr * gr - pi * gi, pr * gi + pi * gr
                    total = (real, imag) if total is None else (total[0] + real, total[1] + imag)
                planes.append(total)
            for c in range(2):
                parts = woven([planes[v][c] for v in (0, 2, 1, 3)])
                for h in range(4):
                    ready[unit, s, c, :, h * lp : (h + 1) * lp] = parts[h]
            if o == half_n - 1:
                for sent in range(half_n):
                    d_copy(kind, unit, sent).start()
            if o == n_dir - 1:
                for sent in range(half_n, n_dir - 1):
                    d_copy(kind, unit, sent).start()
                out[whose(kind, unit)] = ready[unit, s]

    def level_step(step, carry):
        kind, unit = unit_at(step)
        if crossed:
            @pl.when(step == 0)
            def _():
                y_start()

            @pl.when(step == 2 - turned_order)
            def _():
                for i in range(1, plain):
                    x_copy(i).wait_recv()
                    z_start(i, 1)

        for side, present in ((0, has_lower), (1, has_upper)):
            @pl.when(jnp.logical_and(present, step >= crossed))
            def _():
                arrived(side, unit, 1 - x)

        do_unit(kind, unit)

        @pl.when(step < count - 1)
        def _():
            _, following = unit_at(step + 1)
            for side, present in ((0, has_lower), (1, has_upper)):
                @pl.when(present)
                def _():
                    arrived(side, following, x)

            keep_own(following)

        return carry

    _, beginning = unit_at(0)
    for side, present in ((0, has_lower), (1, has_upper)):
        @pl.when(present)
        def _():
            arrived(side, beginning, x)
            if crossed:
                @pl.when(turned_order == 1)
                def _():
                    y_copy(side, x, 1).start()

    keep_own(beginning)
    lax.fori_loop(0, count, level_step, 0)

    def out_arrived(rhs):
        pltpu.make_async_remote_copy(
            ready.at[0, 0], out.at[rhs], ds.at[0, 0], dr.at[rhs],
            (box, across), device_id_type=MESH,
        ).wait_recv()

    for step in range(count):
        kind, unit = unit_at(step)
        for o in range(n_dir - 1):
            d_copy(kind, unit, o).wait_send()
    for o in range(1, n_dir):
        for r in range(plain):
            out_arrived((me + o) % n_dir * count + r)
        if crossed:
            s = (x * half_n + dl + o) % n_dir
            for k in range(2):
                out_arrived((k * half_n + s % half_n) * count + plain + s // half_n)
    for i in range(plain):
        x_copy(i).wait_send()
    if crossed:
        @pl.when(turned_order == 0)
        def _():
            y_first().wait_send()

    for side, sends, gets in ((0, has_upper, has_lower), (1, has_lower, has_upper)):
        @pl.when(sends)
        def _():
            for i in range(plain + crossed):
                for passed in range(2):
                    z_copy(i, passed, side).wait_send()
            if crossed:
                @pl.when(turned_order == 0)
                def _():
                    z_copy(plain, 2, side).wait_send()

        if crossed:
            @pl.when(gets)
            def _():
                y_copy(side, 1 - x, 0).wait_send()

                @pl.when(turned_order == 1)
                def _():
                    y_copy(side, x, 1).wait_send()


def per_device(n_box, n_dir, leaf_patterns, occupancy, pair_lists):
    _, count, _, lt, lp = leaf_patterns.shape
    assert leaf_patterns.shape[0] == 2
    slab = 2 * lt // n_dir
    crossed = int(count == 4 and n_dir % 2 == 0)
    steps = count - crossed
    bf16 = jnp.bfloat16
    lane = np.arange(lp)
    order = []
    for s in range(4):
        h = (lane % 4 - s) % 4
        order.append(lp * h + (lane - h) % lp)
    turn = (order[0] // 4).astype(np.int32)[None]
    first_order = np.concatenate([order[0], order[2]]) // 2
    second_odd = np.concatenate([order[1], order[3]])
    second_order = np.concatenate([order[0], order[2], second_odd])
    high, low = halves(interp_table(lp, 0.0)[first_order[lp:]][:, turn[0]].T)
    c1 = np.concatenate([np.concatenate([high, low], axis=1)] * 2, axis=0)
    row_high, row_low = halves(interp_table(lt, 0.5))
    r1 = np.concatenate([row_high, row_high, row_low], axis=1)
    row_high, row_low = halves(interp_table(2 * lt, 0.5))
    r2 = np.concatenate([row_high, row_high, row_low], axis=1)
    high, low = halves(interp_table(2 * lp, 0.0)[second_odd][:, first_order].T)
    c2 = np.concatenate([high, high, low], axis=0)
    st, _, cp, _ = sines(2 * lt, 2 * lp)
    angle = phase_first * st[:, None] * cp[first_order][None]
    ph1 = np.stack([np.cos(angle), np.sin(angle)]).astype(np.float32)
    st, ct, cp, sp = sines(4 * lt, 4 * lp)
    cp, sp = cp[second_order], sp[second_order]
    angle = phase_second * st[:, None] * sp[None]
    ph2 = np.stack([np.cos(angle), np.sin(angle)]).astype(np.float32)
    polar = np.stack([st, ct])[:, :, None].astype(np.float32)
    azim = np.stack([cp, sp]).astype(np.float32)
    series = series_table(n_box // 2)
    operands = (
        leaf_patterns, occupancy, pair_lists, series, c1, r1, r2, c2, ph1, ph2, polar, azim,
        turn,
    )
    chunk = (2, slab, 4 * lp)
    f32 = jnp.float32
    rows = 2 * lt
    result = pl.pallas_call(
        functools.partial(kernel, (n_box, n_dir, count, lt, lp, slab, crossed)),
        out_shape=jax.ShapeDtypeStruct((n_dir * count,) + chunk, f32),
        in_specs=[pl.BlockSpec(memory_space=pltpu.HBM)] * len(operands),
        out_specs=pl.BlockSpec(memory_space=pltpu.VMEM),
        scratch_shapes=[
            pltpu.VMEM(leaf_patterns.shape, f32),
            pltpu.SMEM(occupancy.shape, jnp.int32),
            pltpu.SMEM(pair_lists.shape, jnp.int32),
            pltpu.SMEM(series.shape, f32),
            pltpu.VMEM(c1.shape, bf16),
            pltpu.VMEM(r1.shape, bf16),
            pltpu.VMEM((1 + crossed, rows) + r2.shape[1:], bf16),
            pltpu.VMEM(c2.shape, bf16),
            pltpu.VMEM(ph1.shape, f32),
            pltpu.VMEM(ph2.shape, f32),
            pltpu.VMEM(polar.shape, f32),
            pltpu.VMEM(azim.shape, f32),
            pltpu.VMEM(turn.shape, jnp.int32),
            pltpu.VMEM((count, 4, lt, lp), f32),
            pltpu.VMEM((steps, 4, lt, lp), f32),
            pltpu.VMEM((4, lt, lp), f32),
            pltpu.VMEM((2, count, 2, 4, lt, lp), f32),
            pltpu.VMEM((2, 2, rows, 2 * lp), f32),
            pltpu.VMEM((2, 4, rows, 4 * lp), bf16),
            pltpu.VMEM((2, 4, rows, 2 * lp), f32),
            pltpu.VMEM((count, n_dir) + chunk, f32),
            pltpu.VMEM((2, 2, 2 * rows, 4 * lp), f32),
            pltpu.SemaphoreType.DMA((len(operands) + 2 * crossed,)),
            pltpu.SemaphoreType.DMA((steps,)),
            pltpu.SemaphoreType.DMA((steps,)),
            pltpu.SemaphoreType.DMA((2, count, 3)),
            pltpu.SemaphoreType.DMA((2, count, 2)),
            pltpu.SemaphoreType.DMA((6,)),
            pltpu.SemaphoreType.DMA((count, n_dir)),
            pltpu.SemaphoreType.DMA((n_dir * count,)),
        ],
        compiler_params=pltpu.CompilerParams(
            collective_id=0, has_side_effects=True, vmem_limit_bytes=48 << 20
        ),
    )(*[pltpu.with_memory_space_constraint(jnp.asarray(operand), pltpu.HBM) for operand in operands])
    return result.reshape(1, 1, n_dir * count, *chunk)


def solution(mesh):
    placed = (P("box", "dir", None, None, None), P("box"), P())
    return jax.shard_map(
        functools.partial(per_device, mesh.shape["box"], mesh.shape["dir"]),
        mesh=mesh,
        in_specs=placed,
        out_specs=P("box", None, None, None, "dir", None),
        check_vma=False,
    )
```
